512 devices in a mesh: bucket: 32 (over x, z), entity: 16 (over y, core).
Axes of the slice: x: 4, y: 8, z: 8, core: 2. Of those that a mesh axis runs over, the one named last changes fastest.
Arguments:
- ent_table: bfloat16 [16384, 512], P('entity'), may hold values from -0.25 to 0.25
- panels: bfloat16 [512, 512, 512], P(('bucket', 'entity')), may hold values from -0.25 to 0.25
- rel_vecs: bfloat16 [512, 512], P(('bucket', 'entity')), may hold values from -0.19921875 to 0.19921875
- head_slots: int32 [512, 2, 128], P(('bucket', 'entity')), may hold values from 0 to 255
- tail_slots: int32 [512, 2, 128], P(('bucket', 'entity')), may hold values from 0 to 255
- negatives: int32 [512, 2, 512], P(('bucket', 'entity')), may hold values from 0 to 255
- requests: int32 [512, 16, 16], P(('bucket', 'entity')), may hold values from 0 to 1023, as said below
- block_count: int32 [512], P(('bucket', 'entity')), may hold values from 1 to 2, as said below
Outputs:
- ent_grad: float32 [16384, 512], P('entity', 'bucket')
- panel_grad: float32 [512, 512, 512], P(('bucket', 'entity'))
- rel_grad: float32 [512, 512], P(('bucket', 'entity'))
The draws below stay inside these ranges and needn't reach their ends.
Inputs may be any that keep to these rules, and one draw needn't show every extreme that they name: `requests`: for each device and row shard the 16 row numbers are distinct. `block_count`: at least one device has exactly 2 live blocks.
All inputs are finite; a program needn't handle non-finite values.
Results may differ from the reference program's by a relative error of at most 0.0095.
Values may be sent and summed in bfloat16 or wider, within the bound.
A program may use at most 64 MiB of HBM per device.

```python
import jax
import jax.numpy as jnp
from jax import lax

D = 512
ENT_DEV = 1024
CAP = 16
BLK_MAX = 2
EDGE = 128
NEG = 512
ENT = 16384
REL = 512
N_BUCKET = 32
N_ENTITY = 16


def draw_requests(key, part):
    pair_count = N_BUCKET * N_ENTITY * N_ENTITY
    subkeys = jax.random.split(jax.random.fold_in(key, 11), pair_count)
    picked = jax.vmap(lambda subkey: jax.random.permutation(subkey, ENT_DEV)[:CAP])(subkeys)
    return picked.reshape(N_BUCKET * N_ENTITY, N_ENTITY, CAP).astype(jnp.int32)


def draw_block_count(key, part):
    device_total = N_BUCKET * N_ENTITY
    base = jax.random.fold_in(key, 23)
    first, second, third = jax.random.split(base, 3)
    picks = jax.random.randint(first, (device_total,), 0, 8)
    lower = jax.random.randint(second, (device_total,), 1, BLK_MAX // 2 + 1)
    counts = jnp.where(picks == 0, BLK_MAX, lower)
    hottest = jax.random.randint(third, (), 0, device_total)
    counts = jnp.where(jnp.arange(device_total) == hottest, BLK_MAX, counts)
    return counts.astype(jnp.int32)


def place_ends(result, key, low, high):
    longest = result.shape.index(max(result.shape))
    spots = []
    for shift in (0, 1):
        where = [jax.random.randint(jax.random.fold_in(key, axis), (), 0, length) for axis, length in enumerate(result.shape)]
        where[longest] = (where[longest] + shift) % result.shape[longest]
        spots.append(tuple(where))
    return result.at[spots[0]].set(low).at[spots[1]].set(high)


def levels(key, extent, shards, least, top_value):
    level = 1.0
    for axis_at, shards_of in shards:
        draws = jax.random.uniform(jax.random.fold_in(jax.random.fold_in(key, 6), axis_at), (shards_of,), jnp.float32, least / len(shards), top_value / len(shards))
        level = level * jnp.repeat(jnp.exp(draws), extent[axis_at] // shards_of).reshape((-1,) + (1,) * (len(extent) - 1 - axis_at))
    return level


def centred(own_key, shape, deviation, reach, cuts=(), held_as=jnp.bfloat16):
    result = deviation * jax.random.normal(own_key, shape, jnp.float32)
    if cuts:
        result = result * levels(own_key, shape, cuts, -0.22, 0.18)
    return jnp.clip(result, -reach, reach).astype(held_as)


def setup_inputs(seed: int = 0) -> dict:
    keys = jax.random.split(jax.random.key(seed), 9)
    ent_table = centred(keys[0], (ENT, D), D ** -0.5, 0.25, ((0, 16),))
    panels = centred(keys[1], (REL, D, D), D ** -0.5, 0.25, ((0, 512),))
    rel_vecs = centred(keys[2], (REL, D), 0.04, 0.19921875, ((0, 512),))
    head_slots = place_ends(jax.random.randint(keys[3], (N_BUCKET * N_ENTITY, BLK_MAX, EDGE), 0, N_ENTITY * CAP), jax.random.fold_in(keys[3], 1), 0, (N_ENTITY * CAP) - 1).astype(jnp.int32)
    tail_slots = place_ends(jax.random.randint(keys[4], (N_BUCKET * N_ENTITY, BLK_MAX, EDGE), 0, N_ENTITY * CAP), jax.random.fold_in(keys[4], 1), 0, (N_ENTITY * CAP) - 1).astype(jnp.int32)
    negatives = place_ends(jax.random.randint(keys[5], (N_BUCKET * N_ENTITY, BLK_MAX, NEG), 0, N_ENTITY * CAP), jax.random.fold_in(keys[5], 1), 0, (N_ENTITY * CAP) - 1).astype(jnp.int32)
    requests = draw_requests(jax.random.fold_in(keys[8], 71), 0)
    block_count = draw_block_count(jax.random.fold_in(keys[8], 71), 0)
    return {"ent_table": ent_table, "panels": panels, "rel_vecs": rel_vecs, "head_slots": head_slots, "tail_slots": tail_slots, "negatives": negatives, "requests": requests, "block_count": block_count}


MARGIN = 2.0


def device_terms(fetched, rel_panel, relation, head_one, tail_one, cand_one, live_mask):
    projected = jnp.dot(fetched, rel_panel.T, preferred_element_type=jnp.float32).astype(jnp.bfloat16)
    feature_count = projected.shape[1]
    head_rows = projected[head_one]
    tail_rows = projected[tail_one]
    cand_rows = projected[cand_one]
    centers = (head_rows.astype(jnp.float32) + relation.astype(jnp.float32)).astype(jnp.bfloat16)
    center_f = centers.astype(jnp.float32)
    tail_f = tail_rows.astype(jnp.float32)
    cand_f = cand_rows.astype(jnp.float32)
    offset = center_f - tail_f
    pos_dist = jnp.sum(offset * offset, -1)
    pos_weight = jax.nn.sigmoid(pos_dist - MARGIN) * live_mask[:, None]
    cross_terms = jnp.einsum("bed,bnd->ben", center_f, cand_f)
    neg_dist = jnp.sum(center_f * center_f, -1)[:, :, None] + jnp.sum(cand_f * cand_f, -1)[:, None, :] - 2.0 * cross_terms
    neg_weight = -jax.nn.sigmoid(MARGIN - neg_dist) / NEG * live_mask[:, None, None]
    weight_b = lax.optimization_barrier(neg_weight.astype(jnp.bfloat16)).astype(jnp.float32)
    grad_center = (2.0 * pos_weight[..., None] * offset
                   + 2.0 * jnp.sum(neg_weight, -1)[..., None] * center_f
                   - 2.0 * jnp.einsum("ben,bnd->bed", weight_b, cand_f))
    grad_tail = -2.0 * pos_weight[..., None] * offset
    grad_cand = (2.0 * jnp.sum(neg_weight, 1)[..., None] * cand_f
                 - 2.0 * jnp.einsum("ben,bed->bnd", weight_b, center_f))
    grad_proj = jnp.zeros(projected.shape, jnp.float32)
    grad_proj = grad_proj.at[head_one.reshape(-1)].add(grad_center.reshape(-1, feature_count))
    grad_proj = grad_proj.at[tail_one.reshape(-1)].add(grad_tail.reshape(-1, feature_count))
    grad_proj = grad_proj.at[cand_one.reshape(-1)].add(grad_cand.reshape(-1, feature_count))
    grad_rel = jnp.sum(grad_center, (0, 1))
    grad_proj_b = grad_proj.astype(jnp.bfloat16)
    grad_fetched = jnp.dot(grad_proj_b, rel_panel, preferred_element_type=jnp.float32)
    grad_panel = jnp.dot(grad_proj_b.T, fetched, preferred_element_type=jnp.float32)
    return grad_fetched, grad_panel, grad_rel


def reference(ent_table, panels, rel_vecs, head_slots, tail_slots, negatives, requests, block_count):
    device_total = N_BUCKET * N_ENTITY
    owners = jnp.arange(N_ENTITY, dtype=jnp.int32)[:, None] * ENT_DEV

    def visit(grad_table, device_index):
        row_numbers = (owners + requests[device_index]).reshape(-1).astype(jnp.int32)
        fetched = ent_table[row_numbers]
        live_mask = (jnp.arange(BLK_MAX, dtype=jnp.int32) < block_count[device_index]).astype(jnp.float32)
        grad_rows, grad_panel, grad_rel = device_terms(
            fetched, panels[device_index], rel_vecs[device_index],
            head_slots[device_index], tail_slots[device_index], negatives[device_index], live_mask)
        return grad_table.at[row_numbers].add(grad_rows), (grad_panel, grad_rel)

    grad_table, outputs = lax.scan(visit, jnp.zeros((ENT, D), jnp.float32),
                                   jnp.arange(device_total, dtype=jnp.int32))
    return grad_table, outputs[0], outputs[1]
```

```python
import functools

import jax
import jax.numpy as jnp
from jax import lax
from jax.experimental import pallas as pl
from jax.experimental.pallas import tpu as pltpu
from jax.sharding import PartitionSpec as P

MARGIN = 2.0
LANES = 128
MESH = pl.DeviceIdType.MESH
BF = jnp.bfloat16
F32 = jnp.float32


def mm(a, b):
    return jnp.dot(a, b, preferred_element_type=F32)


def mm_nt(a, b):
    return lax.dot_general(a, b, (((1,), (1,)), ((), ())), preferred_element_type=F32)


def iota(shape, axis):
    return lax.broadcasted_iota(jnp.int32, shape, axis)


def to_col(row):
    n = row.shape[1]
    eye = iota((n, n), 0) == iota((n, n), 1)
    return jnp.sum(jnp.where(eye, row, 0.0), axis=1, keepdims=True)


def to_row(col):
    n = col.shape[0]
    eye = iota((n, n), 0) == iota((n, n), 1)
    return jnp.sum(jnp.where(eye, col, 0.0), axis=0, keepdims=True)


def one_hot(row, n):
    return (iota((n, row.shape[1]), 0) == row).astype(F32)


def local_terms(fetched, panel, rel, head_ref, tail_ref, neg_ref, live_count):
    blocks, edge = head_ref.shape
    neg = neg_ref.shape[1]
    slots = fetched.shape[0]
    edges = blocks * edge
    proj = mm_nt(fetched, panel).astype(BF)
    proj_f = proj.astype(F32)
    head = jnp.concatenate([head_ref[j : j + 1, :] for j in range(blocks)], axis=1)
    tail = jnp.concatenate([tail_ref[j : j + 1, :] for j in range(blocks)], axis=1)
    head_t = one_hot(head, slots)
    tail_t = one_hot(tail, slots)
    block_of = iota((edges, 1), 0) // edge
    live = (block_of < live_count).astype(F32)
    count = jnp.zeros((edges, slots), F32)
    for j in range(blocks):
        hits = jnp.sum(one_hot(neg_ref[j : j + 1, :], slots), axis=1, keepdims=True)
        count = jnp.where(block_of == j, to_row(hits), count)

    centers = (mm(head_t.T.astype(BF), proj) + rel).astype(BF)
    center_f = centers.astype(F32)
    offset = center_f - mm(tail_t.T.astype(BF), proj)
    pos_weight = jax.nn.sigmoid(jnp.sum(offset * offset, axis=1, keepdims=True) - MARGIN) * live
    proj_sq = to_row(jnp.sum(proj_f * proj_f, axis=1, keepdims=True))
    center_sq = jnp.sum(center_f * center_f, axis=1, keepdims=True)
    dist = center_sq + proj_sq - 2.0 * mm_nt(centers, proj)
    weight = -jax.nn.sigmoid(MARGIN - dist) * (live * (1.0 / neg)) * count
    weight_t = weight.T
    pulled = 2.0 * pos_weight * offset
    grad_center = (
        pulled
        + 2.0 * jnp.sum(weight, axis=1, keepdims=True) * center_f
        - 2.0 * mm(weight.astype(BF), proj)
    )
    grad_proj = (
        mm(head_t.astype(BF), grad_center.astype(BF))
        - mm(tail_t.astype(BF), pulled.astype(BF))
        + 2.0 * jnp.sum(weight_t, axis=1, keepdims=True) * proj_f
        - 2.0 * mm(weight_t.astype(BF), centers)
    ).astype(BF)
    return grad_proj, jnp.sum(grad_center, axis=0, keepdims=True)


def kernel(
    nb, ne,
    table_hbm, panel_hbm, rel_ref, head_ref, tail_ref, neg_ref, req_ref, count_ref,
    ent_ref, proj_out, fetched_out, rel_out,
    table, panel, msg, reqbuf, asked_all, rows, fetched, gf, grecv, gt, frecv, spread, hot,
    lsem, qs, qr, as_, ar, cs, cr, es, er, fs, fr,
):
    b = lax.axis_index("bucket")
    e = lax.axis_index("entity")
    cap = req_ref.shape[1]
    slots = ne * cap
    width = frecv.shape[2]
    halves = frecv.shape[1]
    per_half = ne // halves
    table_rows = table.shape[0]

    load_table = pltpu.make_async_copy(table_hbm, table, lsem.at[0])
    load_panel = pltpu.make_async_copy(panel_hbm, panel, lsem.at[1])
    load_table.start()
    load_panel.start()

    def entity_peer(j):
        return lax.rem(e + j, ne)

    def bucket_peer(i):
        return lax.rem(b + i, nb)

    def each(lo, hi, do):
        def step(k, carry):
            do(k)
            return carry

        lax.fori_loop(lo, hi, step, 0)

    barrier = pltpu.get_barrier_semaphore()
    each(1, ne, lambda j: pl.semaphore_signal(
        barrier, inc=1, device_id={"entity": entity_peer(j)}, device_id_type=MESH))
    each(1, nb, lambda i: pl.semaphore_signal(
        barrier, inc=1, device_id={"bucket": bucket_peer(i)}, device_id_type=MESH))

    req = req_ref[...]
    repeat = (iota((cap, slots), 0) == lax.rem(iota((cap, slots), 1), cap)).astype(BF)
    high = mm((req >> 5).astype(F32).astype(BF), repeat)
    low = mm((req & 31).astype(F32).astype(BF), repeat)
    tiled = (high * 32.0 + low).astype(jnp.int32)
    slot_of = lax.rem(iota((ne, slots), 0) - e + ne, ne)
    tiled = jnp.where(iota((ne, slots), 1) // cap == slot_of, tiled, 0)
    for o in range(ne):
        msg[o] = tiled[o : o + 1, :]

    pl.semaphore_wait(barrier, ne + nb - 2)

    def request_copy(j):
        return pltpu.make_async_remote_copy(
            src_ref=msg.at[entity_peer(j)], dst_ref=reqbuf.at[j], send_sem=qs.at[j],
            recv_sem=qr.at[j], device_id={"entity": entity_peer(j)}, device_id_type=MESH)

    each(1, ne, lambda j: request_copy(j).start())
    reqbuf[0] = msg[e]
    each(1, ne, lambda j: request_copy(j).wait())
    asked = reqbuf[0]
    for j in range(1, ne):
        asked = asked + reqbuf[j]
    asked_all[0] = asked

    def asked_copy(i):
        return pltpu.make_async_remote_copy(
            src_ref=asked_all.at[0], dst_ref=asked_all.at[i], send_sem=as_.at[i],
            recv_sem=ar.at[i], device_id={"bucket": bucket_peer(i)}, device_id_type=MESH)

    load_table.wait()
    asked_col = to_col(asked.astype(F32)).astype(jnp.int32)
    pick = (iota((slots, table_rows), 1) == asked_col).astype(F32).astype(BF)
    rows[...] = mm(pick, table[...]).astype(BF)

    def at_slot(o):
        return pl.ds(pl.multiple_of(o * cap, cap), cap)

    def row_copy(j):
        return pltpu.make_async_remote_copy(
            src_ref=rows.at[at_slot(j)], dst_ref=fetched.at[at_slot(e)], send_sem=cs.at[j],
            recv_sem=cr.at[j], device_id={"entity": lax.rem(e - j + ne, ne)}, device_id_type=MESH)

    each(1, ne, lambda j: row_copy(j).start())
    each(1, nb, lambda i: asked_copy(i).start())
    fetched[at_slot(e), :] = rows[0:cap, :]
    load_panel.wait()
    each(1, ne, lambda j: row_copy(j).wait())

    grad_proj, grad_rel = local_terms(
        fetched[...], panel[...], rel_ref[...].astype(F32), head_ref, tail_ref, neg_ref, count_ref[0])
    gf[...] = mm(grad_proj, panel[...]).astype(BF)

    def grad_copy(j):
        return pltpu.make_async_remote_copy(
            src_ref=gf.at[at_slot(entity_peer(j))], dst_ref=grecv.at[at_slot(j)],
            send_sem=es.at[j], recv_sem=er.at[j],
            device_id={"entity": entity_peer(j)}, device_id_type=MESH)

    each(1, ne, lambda j: grad_copy(j).start())
    grecv[0:cap, :] = gf[at_slot(e), :]
    rel_out[...] = grad_rel
    proj_out[...] = grad_proj
    fetched_out[...] = fetched[...]

    each(1, nb, lambda i: asked_copy(i).wait())
    for i in range(nb):
        hi = asked_all[i] & (LANES - 1)
        hot[:, i * slots : (i + 1) * slots] = one_hot(hi, LANES).astype(BF)

    def part_copy(h, i):
        return pltpu.make_async_remote_copy(
            src_ref=gt.at[h, pl.ds(pl.multiple_of(bucket_peer(i) * width, width), width), :],
            dst_ref=frecv.at[i, h], send_sem=fs.at[h, i], recv_sem=fr.at[h, i],
            device_id={"bucket": bucket_peer(i)}, device_id_type=MESH)

    for h in range(halves):
        first = h * per_half
        each(max(first, 1), first + per_half, lambda j: grad_copy(j).wait())
        piece = grecv[first * cap : (first + per_half) * cap, :].astype(F32)
        gt[h] = piece.T.astype(BF)
        each(1, nb, lambda i, h=h: part_copy(h, i).start())
        frecv[0, h] = gt[h, pl.ds(pl.multiple_of(b * width, width), width), :]

    high_rows = table_rows // LANES
    half_lanes = per_half * cap
    for i in range(nb):
        for h in range(halves):
            if i:
                part_copy(h, i).wait()
            at = i * slots + h * half_lanes
            lo = asked_all[i, :, h * half_lanes : (h + 1) * half_lanes] >> 7
            g = frecv[i, h].astype(F32)
            spread[:, at : at + half_lanes] = jnp.concatenate(
                [jnp.where(lo == k, g, 0.0) for k in range(high_rows)], axis=0).astype(BF)
    total = mm_nt(spread[...], hot[...])
    for k in range(high_rows):
        ent_ref[:, k * LANES : (k + 1) * LANES] = total[k * width : (k + 1) * width, :]


def body(ent_table, panels, rel_vecs, head_slots, tail_slots, negatives, requests, block_count):
    nb = lax.axis_size("bucket")
    ne = lax.axis_size("entity")
    rows, feat = ent_table.shape
    cap = requests.shape[2]
    slots = ne * cap
    width = feat // nb
    halves = 2
    vmem = pl.BlockSpec(memory_space=pltpu.VMEM)
    anywhere = pl.BlockSpec(memory_space=pl.ANY)
    smem = pl.BlockSpec(memory_space=pltpu.SMEM)
    dma = pltpu.SemaphoreType.DMA
    ent_t, grad_proj, fetched, grad_rel = pl.pallas_call(
        functools.partial(kernel, nb, ne),
        out_shape=(
            jax.ShapeDtypeStruct((width, rows), F32),
            jax.ShapeDtypeStruct((slots, feat), BF),
            jax.ShapeDtypeStruct((slots, feat), BF),
            jax.ShapeDtypeStruct((1, feat), F32),
        ),
        in_specs=[anywhere, anywhere, vmem, vmem, vmem, vmem, vmem, smem],
        out_specs=(vmem, vmem, vmem, vmem),
        scratch_shapes=[
            pltpu.VMEM((rows, feat), BF),
            pltpu.VMEM((feat, feat), BF),
            pltpu.VMEM((ne, 1, slots), jnp.int32),
            pltpu.VMEM((ne, 1, slots), jnp.int32),
            pltpu.VMEM((nb, 1, slots), jnp.int32),
            pltpu.VMEM((slots, feat), BF),
            pltpu.VMEM((slots, feat), BF),
            pltpu.VMEM((slots, feat), BF),
            pltpu.VMEM((slots, feat), BF),
            pltpu.VMEM((halves, feat, slots // halves), BF),
            pltpu.VMEM((nb, halves, width, slots // halves), BF),
            pltpu.VMEM((rows // LANES * width, nb * slots), BF),
            pltpu.VMEM((LANES, nb * slots), BF),
            dma((2,)),
            dma((ne,)), dma((ne,)),
            dma((nb,)), dma((nb,)),
            dma((ne,)), dma((ne,)),
            dma((ne,)), dma((ne,)),
            dma((halves, nb)), dma((halves, nb)),
        ],
        compiler_params=pltpu.CompilerParams(
            collective_id=0, has_side_effects=True, vmem_limit_bytes=48 * 1024 * 1024
        ),
        name="transr",
    )(
        ent_table, panels[0], rel_vecs, head_slots[0], tail_slots[0], negatives[0],
        requests[0], block_count,
    )
    grad_panel = jnp.einsum("kd,ke->de", grad_proj, fetched, preferred_element_type=F32)
    return (ent_t.T, grad_panel[None], grad_rel)


def solution(mesh):
    both = ("bucket", "entity")
    placed = (
        P("entity", None),
        P(both, None, None),
        P(both, None),
        P(both, None, None),
        P(both, None, None),
        P(both, None, None),
        P(both, None, None),
        P(both),
    )
    return jax.shard_map(
        body,
        mesh=mesh,
        in_specs=placed,
        out_specs=(P("entity", "bucket"), P(both, None, None), P(both, None)),
        check_vma=False,
    )
```

```python
import functools

import jax
import jax.numpy as jnp
from jax import lax
from jax.experimental import pallas as pl
from jax.experimental.pallas import tpu as pltpu
from jax.sharding import PartitionSpec as P

MARGIN = 2.0
LANES = 128
HALVES = 2
X_SIZE = 4
MESH = pl.DeviceIdType.MESH
BF = jnp.bfloat16
F32 = jnp.float32


def mm(a, b):
    return jnp.dot(a, b, preferred_element_type=F32)


def mm_nt(a, b):
    return lax.dot_general(a, b, (((1,), (1,)), ((), ())), preferred_element_type=F32)


def mm_tn(a, b):
    return lax.dot_general(a, b, (((0,), (0,)), ((), ())), preferred_element_type=F32)


def iota(shape, axis):
    return lax.broadcasted_iota(jnp.int32, shape, axis)


def to_col(row):
    n = row.shape[1]
    eye = iota((n, n), 0) == iota((n, n), 1)
    return jnp.sum(jnp.where(eye, row, 0.0), axis=1, keepdims=True)


def to_row(col):
    n = col.shape[0]
    eye = iota((n, n), 0) == iota((n, n), 1)
    return jnp.sum(jnp.where(eye, col, 0.0), axis=0, keepdims=True)


def one_hot(row, n):
    return (iota((n, row.shape[1]), 0) == row).astype(F32)


def slot_tables(head_ref, tail_ref, neg_ref, live_count, slots):
    blocks, edge = head_ref.shape
    edges = blocks * edge
    head = jnp.concatenate([head_ref[j : j + 1, :] for j in range(blocks)], axis=1)
    tail = jnp.concatenate([tail_ref[j : j + 1, :] for j in range(blocks)], axis=1)
    head_t = one_hot(head, slots)
    tail_t = one_hot(tail, slots)
    block_of = iota((edges, 1), 0) // edge
    live = (block_of < live_count).astype(F32)
    count = jnp.zeros((edges, slots), F32)
    for j in range(blocks):
        hits = jnp.sum(one_hot(neg_ref[j : j + 1, :], slots), axis=1, keepdims=True)
        count = jnp.where(block_of == j, to_row(hits), count)
    count = count * (live * (1.0 / neg_ref.shape[1]))
    return head_t.astype(BF), tail_t.astype(BF), head_t.T.astype(BF), tail_t.T.astype(BF), live, count


def local_terms(fetched, panel, rel, tables):
    head_t, tail_t, head, tail, live, count = tables
    proj = mm_nt(fetched, panel).astype(BF)
    proj_f = proj.astype(F32)
    centers = (mm(head, proj) + rel).astype(BF)
    center_f = centers.astype(F32)
    offset = center_f - mm(tail, proj)
    pos_weight = jax.nn.sigmoid(jnp.sum(offset * offset, axis=1, keepdims=True) - MARGIN) * live
    proj_sq = to_row(jnp.sum(proj_f * proj_f, axis=1, keepdims=True))
    center_sq = jnp.sum(center_f * center_f, axis=1, keepdims=True)
    dist = center_sq + proj_sq - 2.0 * mm_nt(centers, proj)
    weight = -jax.nn.sigmoid(MARGIN - dist) * count
    weight_t = weight.T
    pulled = 2.0 * pos_weight * offset
    grad_center = (
        pulled
        + 2.0 * jnp.sum(weight, axis=1, keepdims=True) * center_f
        - 2.0 * mm(weight.astype(BF), proj)
    )
    grad_proj = (
        mm(head_t, grad_center.astype(BF))
        - mm(tail_t, pulled.astype(BF))
        + 2.0 * jnp.sum(weight_t, axis=1, keepdims=True) * proj_f
        - 2.0 * mm(weight_t.astype(BF), centers)
    ).astype(BF)
    return grad_proj, jnp.sum(grad_center, axis=0, keepdims=True)


def away(step, size):
    return min(step, size - step)


def kernel(
    nb, ne,
    table_hbm, panel_hbm, rel_hbm, head_hbm, tail_hbm, neg_hbm, req_hbm, count_ref,
    ent_ref, proj_out, fetched_out, rel_out,
    table, panel, rel_v, head_v, tail_v, neg_v, req_v, wide,
    msg, reqbuf, asked_all, rows, fetched, gf, grecv, gt, frecv, spread, hot,
    lsem, qs, qr, as_, ar, cs, cr, es, er, fs, fr,
):
    b = lax.axis_index("bucket")
    e = lax.axis_index("entity")
    cap = req_v.shape[1]
    slots = ne * cap
    width = frecv.shape[2]
    per_half = ne // HALVES
    half_lanes = per_half * cap
    table_rows = table.shape[0]
    high_rows = table_rows // LANES

    chips = ne // 2
    steps = sorted(range(chips), key=lambda d: away(d, chips))

    def ahead(s):
        return 2 * ((e // 2 + steps[s // 2]) & (chips - 1)) + ((e + s) & 1)

    def behind(s):
        return 2 * ((e // 2 - steps[s // 2]) & (chips - 1)) + ((e + s) & 1)

    zs = nb // X_SIZE
    far_first = sorted(
        range(1, nb), key=lambda i: -(away(i // zs, X_SIZE) + away(i % zs, zs)))

    def bucket_peer(i):
        return ((b // zs + i // zs) & (X_SIZE - 1)) * zs + ((b + i) & (zs - 1))

    def signal(where):
        pl.semaphore_signal(barrier, inc=1, device_id=where, device_id_type=MESH)

    def send(src, dst, sems, where):
        return pltpu.make_async_remote_copy(
            src_ref=src, dst_ref=dst, send_sem=sems[0], recv_sem=sems[1],
            device_id=where, device_id_type=MESH)

    barrier = pltpu.get_barrier_semaphore()
    for s in reversed(range(1, ne)):
        signal({"entity": ahead(s)})
    loads = [
        pltpu.make_async_copy(src, dst, lsem.at[k])
        for k, (src, dst) in enumerate([
            (req_hbm, req_v), (table_hbm, table), (head_hbm, head_v), (tail_hbm, tail_v),
            (neg_hbm, neg_v), (rel_hbm, rel_v), (panel_hbm, panel),
        ])
    ]
    for load in loads:
        load.start()
    for i in far_first:
        signal({"bucket": bucket_peer(i)})

    loads[0].wait()
    req = req_v[...]
    repeat = (iota((cap, slots), 0) == lax.rem(iota((cap, slots), 1), cap)).astype(F32).astype(BF)
    high = mm((req >> 5).astype(F32).astype(BF), repeat)
    low = mm((req & 31).astype(F32).astype(BF), repeat)
    wide[...] = (high * 32.0 + low).astype(jnp.int32)
    for s in range(ne):
        mine = iota((1, slots), 1) // cap == s
        msg[s] = jnp.where(mine, wide[pl.ds(ahead(s), 1), :], 0)

    pl.semaphore_wait(barrier, ne + nb - 2)

    asks = {
        s: send(msg.at[s], reqbuf.at[s], (qs.at[s], qr.at[s]), {"entity": ahead(s)})
        for s in range(1, ne)
    }
    for s in reversed(range(1, ne)):
        asks[s].start()
    loads[1].wait()
    asked = msg[0]
    for s in range(1, ne):
        asks[s].wait()
        asked = asked + reqbuf[s]
    asked_all[0] = asked

    asked_col = to_col(asked.astype(F32)).astype(jnp.int32)
    pick = (iota((slots, table_rows), 1) == asked_col).astype(F32).astype(BF)
    rows[...] = mm(pick, table[...]).astype(BF)

    def at_slot(s):
        return slice(s * cap, (s + 1) * cap)

    def at_entity(o):
        return pl.ds(pl.multiple_of(o * cap, cap), cap)

    returns = {
        s: send(rows.at[at_slot(s)], fetched.at[at_entity(e)], (cs.at[s], cr.at[s]),
                {"entity": behind(s)})
        for s in range(1, ne)
    }
    for s in reversed(range(1, ne)):
        returns[s].start()
    lists = {
        i: send(asked_all.at[0], asked_all.at[i], (as_.at[i], ar.at[i]), {"bucket": bucket_peer(i)})
        for i in range(1, nb)
    }
    for i in far_first:
        lists[i].start()
    fetched[at_entity(e), :] = rows[at_slot(0), :]

    for load in loads[2:]:
        load.wait()
    tables = slot_tables(head_v, tail_v, neg_v, count_ref[0], slots)
    for s in range(1, ne):
        returns[s].wait()

    grad_proj, grad_rel = local_terms(fetched[...], panel[...], rel_v[...].astype(F32), tables)
    gf[...] = mm(grad_proj, panel[...]).astype(BF)

    grads = {
        s: send(gf.at[at_entity(ahead(s))], grecv.at[at_slot(s)], (es.at[s], er.at[s]),
                {"entity": ahead(s)})
        for s in range(1, ne)
    }
    for h in range(HALVES):
        for s in reversed(range(max(h * per_half, 1), (h + 1) * per_half)):
            grads[s].start()
    grecv[at_slot(0), :] = gf[at_entity(e), :]
    rel_out[...] = grad_rel
    proj_out[...] = grad_proj
    fetched_out[...] = fetched[...]

    def part(h, i):
        at = pl.ds(pl.multiple_of(bucket_peer(i) * width, width), width)
        return send(gt.at[h, at, :], frecv.at[h, i], (fs.at[h, i], fr.at[h, i]),
                    {"bucket": bucket_peer(i)})

    for h in range(HALVES):
        for s in range(max(h * per_half, 1), (h + 1) * per_half):
            grads[s].wait()
        piece = grecv[h * half_lanes : (h + 1) * half_lanes, :].astype(F32)
        gt[h] = piece.T.astype(BF)
        for i in far_first:
            part(h, i).start()
        frecv[h, 0] = gt[h, pl.ds(pl.multiple_of(b * width, width), width), :]
        if h == 0:
            for i in range(1, nb):
                lists[i].wait()
            for i in range(nb):
                for k in range(HALVES):
                    hi = asked_all[i, :, k * half_lanes : (k + 1) * half_lanes] & (LANES - 1)
                    hot[k, :, i * half_lanes : (i + 1) * half_lanes] = one_hot(hi, LANES).astype(BF)

    total = None
    for h in range(HALVES):
        for i in [0] + far_first[::-1]:
            if i:
                part(h, i).wait()
            lo = asked_all[i, :, h * half_lanes : (h + 1) * half_lanes] >> 7
            g = frecv[h, i].astype(F32)
            spread[h, :, i * half_lanes : (i + 1) * half_lanes] = jnp.concatenate(
                [jnp.where(lo == k, g, 0.0) for k in range(high_rows)], axis=0).astype(BF)
        share = mm_nt(spread[h], hot[h])
        total = share if total is None else total + share
    for k in range(high_rows):
        ent_ref[:, k * LANES : (k + 1) * LANES] = total[k * width : (k + 1) * width, :]


def finish(ent_ref, proj_ref, fetched_ref, rel_ref, ent_out, panel_out, rel_out, held, sem):
    outs = [
        pltpu.make_async_copy(ent_ref, ent_out, sem.at[0]),
        pltpu.make_async_copy(rel_ref, rel_out, sem.at[1]),
    ]
    for out in outs:
        out.start()
    half = held.shape[0] // 2
    for h in range(2):
        part = slice(h * half, (h + 1) * half)
        held[part, :] = mm_tn(proj_ref[:, part], fetched_ref[...])
        out = pltpu.make_async_copy(held.at[part], panel_out.at[part], sem.at[2 + h])
        out.start()
        outs.append(out)
    for out in outs:
        out.wait()


def body(ent_table, panels, rel_vecs, head_slots, tail_slots, negatives, requests, block_count):
    nb = lax.axis_size("bucket")
    ne = lax.axis_size("entity")
    rows, feat = ent_table.shape
    cap = requests.shape[2]
    slots = ne * cap
    width = feat // nb
    half = slots // HALVES
    vmem = pl.BlockSpec(memory_space=pltpu.VMEM)
    hbm = pl.BlockSpec(memory_space=pltpu.HBM)
    dma = pltpu.SemaphoreType.DMA
    shapes = (
        jax.ShapeDtypeStruct((width, rows), F32),
        jax.ShapeDtypeStruct((slots, feat), BF),
        jax.ShapeDtypeStruct((slots, feat), BF),
        jax.ShapeDtypeStruct((1, feat), F32),
    )
    ent_t, grad_proj, fetched, grad_rel = pl.pallas_call(
        functools.partial(kernel, nb, ne),
        out_shape=shapes,
        in_specs=[hbm] * 7 + [pl.BlockSpec(memory_space=pltpu.SMEM)],
        out_specs=(vmem,) * 4,
        scratch_shapes=[
            pltpu.VMEM((rows, feat), BF),
            pltpu.VMEM((feat, feat), BF),
            pltpu.VMEM(rel_vecs.shape, BF),
            pltpu.VMEM(head_slots.shape[1:], jnp.int32),
            pltpu.VMEM(tail_slots.shape[1:], jnp.int32),
            pltpu.VMEM(negatives.shape[1:], jnp.int32),
            pltpu.VMEM(requests.shape[1:], jnp.int32),
            pltpu.VMEM((ne, slots), jnp.int32),
            pltpu.VMEM((ne, 1, slots), jnp.int32),
            pltpu.VMEM((ne, 1, slots), jnp.int32),
            pltpu.VMEM((nb, 1, slots), jnp.int32),
            pltpu.VMEM((slots, feat), BF),
            pltpu.VMEM((slots, feat), BF),
            pltpu.VMEM((slots, feat), BF),
            pltpu.VMEM((slots, feat), BF),
            pltpu.VMEM((HALVES, feat, half), BF),
            pltpu.VMEM((HALVES, nb, width, half), BF),
            pltpu.VMEM((HALVES, rows // LANES * width, nb * half), BF),
            pltpu.VMEM((HALVES, LANES, nb * half), BF),
            dma((7,)),
            dma((ne,)), dma((ne,)),
            dma((nb,)), dma((nb,)),
            dma((ne,)), dma((ne,)),
            dma((ne,)), dma((ne,)),
            dma((HALVES, nb)), dma((HALVES, nb)),
        ],
        compiler_params=pltpu.CompilerParams(
            collective_id=0, has_side_effects=True, vmem_limit_bytes=40 * 1024 * 1024
        ),
        name="transr",
    )(
        *(pltpu.with_memory_space_constraint(x, pltpu.HBM) for x in (
            ent_table, panels[0], rel_vecs, head_slots[0], tail_slots[0], negatives[0],
            requests[0])),
        block_count,
    )
    ent_t, grad_panel, grad_rel = pl.pallas_call(
        finish,
        out_shape=(shapes[0], jax.ShapeDtypeStruct((feat, feat), F32), shapes[3]),
        in_specs=[vmem] * 4,
        out_specs=(hbm,) * 3,
        scratch_shapes=[pltpu.VMEM((feat, feat), F32), dma((4,))],
        compiler_params=pltpu.CompilerParams(vmem_limit_bytes=8 * 1024 * 1024),
        name="finish",
    )(ent_t, grad_proj, fetched, grad_rel)
    return (ent_t.T, grad_panel[None], grad_rel)


def solution(mesh):
    both = ("bucket", "entity")
    placed = (
        P("entity", None),
        P(both, None, None),
        P(both, None),
        P(both, None, None),
        P(both, None, None),
        P(both, None, None),
        P(both, None, None),
        P(both),
    )
    return jax.shard_map(
        body,
        mesh=mesh,
        in_specs=placed,
        out_specs=(P("entity", "bucket"), P(both, None, None), P(both, None)),
        check_vma=False,
    )
```

```python
import functools

import jax
import jax.numpy as jnp
from jax import lax
from jax.experimental import pallas as pl
from jax.experimental.pallas import tpu as pltpu
from jax.sharding import PartitionSpec as P

MARGIN = 2.0
LANES = 128
HALVES = 2
GROUPS = 4
X_SIZE = 4
MESH = pl.DeviceIdType.MESH
BF = jnp.bfloat16
F32 = jnp.float32


def mm(a, b):
    return jnp.dot(a, b, preferred_element_type=F32)


def mm_nt(a, b):
    return lax.dot_general(a, b, (((1,), (1,)), ((), ())), preferred_element_type=F32)


def mm_tn(a, b):
    return lax.dot_general(a, b, (((0,), (0,)), ((), ())), preferred_element_type=F32)


def iota(shape, axis):
    return lax.broadcasted_iota(jnp.int32, shape, axis)


def to_col(row):
    n = row.shape[1]
    eye = iota((n, n), 0) == iota((n, n), 1)
    return jnp.sum(jnp.where(eye, row, 0.0), axis=1, keepdims=True)


def to_row(col):
    n = col.shape[0]
    eye = iota((n, n), 0) == iota((n, n), 1)
    return jnp.sum(jnp.where(eye, col, 0.0), axis=0, keepdims=True)


def one_hot(row, n):
    return (iota((n, row.shape[1]), 0) == row).astype(F32)


def slot_tables(head_ref, tail_ref, neg_ref, live_count, slots):
    blocks, edge = head_ref.shape
    edges = blocks * edge
    head = jnp.concatenate([head_ref[j : j + 1, :] for j in range(blocks)], axis=1)
    tail = jnp.concatenate([tail_ref[j : j + 1, :] for j in range(blocks)], axis=1)
    head_t = one_hot(head, slots)
    tail_t = one_hot(tail, slots)
    block_of = iota((edges, 1), 0) // edge
    live = (block_of < live_count).astype(F32)
    count = jnp.zeros((edges, slots), F32)
    for j in range(blocks):
        hits = jnp.sum(one_hot(neg_ref[j : j + 1, :], slots), axis=1, keepdims=True)
        count = jnp.where(block_of == j, to_row(hits), count)
    count = count * (live * (1.0 / neg_ref.shape[1]))
    return head_t.astype(BF), tail_t.astype(BF), head_t.T.astype(BF), tail_t.T.astype(BF), live, count


def local_terms(fetched, panel, rel, tables):
    head_t, tail_t, head, tail, live, count = tables
    proj = mm_nt(fetched, panel).astype(BF)
    proj_f = proj.astype(F32)
    centers = (mm(head, proj) + rel).astype(BF)
    center_f = centers.astype(F32)
    offset = center_f - mm(tail, proj)
    pos_weight = jax.nn.sigmoid(jnp.sum(offset * offset, axis=1, keepdims=True) - MARGIN) * live
    proj_sq = to_row(jnp.sum(proj_f * proj_f, axis=1, keepdims=True))
    center_sq = jnp.sum(center_f * center_f, axis=1, keepdims=True)
    dist = center_sq + proj_sq - 2.0 * mm_nt(centers, proj)
    weight = -jax.nn.sigmoid(MARGIN - dist) * count
    weight_t = weight.T
    pulled = 2.0 * pos_weight * offset
    grad_center = (
        pulled
        + 2.0 * jnp.sum(weight, axis=1, keepdims=True) * center_f
        - 2.0 * mm(weight.astype(BF), proj)
    )
    grad_proj = (
        mm(head_t, grad_center.astype(BF))
        - mm(tail_t, pulled.astype(BF))
        + 2.0 * jnp.sum(weight_t, axis=1, keepdims=True) * proj_f
        - 2.0 * mm(weight_t.astype(BF), centers)
    ).astype(BF)
    return grad_proj, jnp.sum(grad_center, axis=0, keepdims=True)


def away(step, size):
    return min(step, size - step)


def kernel(
    nb, ne,
    table_hbm, panel_hbm, rel_hbm, head_hbm, tail_hbm, neg_hbm, req_hbm, count_ref,
    ent_ref, proj_out, fetched_out, rel_out,
    table, panel, rel_v, head_v, tail_v, neg_v, req_v, wide,
    msg, reqbuf, asked_all, rows, fetched, gf, grecv, gt, frecv, spread, hot,
    lsem, ask_sem, list_sem, row_sem, grad_sem, part_sem,
):
    b = lax.axis_index("bucket")
    e = lax.axis_index("entity")
    cap = req_v.shape[1]
    slots = ne * cap
    width = frecv.shape[2]
    per_half = ne // HALVES
    half_lanes = per_half * cap
    table_rows = table.shape[0]
    high_rows = table_rows // LANES

    chips = ne // 2
    steps = sorted(range(chips), key=lambda d: away(d, chips))

    def ahead(s):
        return 2 * ((e // 2 + steps[s // 2]) & (chips - 1)) + ((e + s) & 1)

    def behind(s):
        return 2 * ((e // 2 - steps[s // 2]) & (chips - 1)) + ((e + s) & 1)

    zs = nb // X_SIZE
    far_first = sorted(
        range(1, nb), key=lambda i: -(away(i // zs, X_SIZE) + away(i % zs, zs)))

    def bucket_peer(i):
        return ((b // zs + i // zs) & (X_SIZE - 1)) * zs + ((b + i) & (zs - 1))

    def signal(where):
        pl.semaphore_signal(barrier, inc=1, device_id=where, device_id_type=MESH)

    def send(src, dst, sent, arrived, where):
        return pltpu.make_async_remote_copy(
            src_ref=src, dst_ref=dst, send_sem=sent, recv_sem=arrived,
            device_id=where, device_id_type=MESH)

    def whole(ref, sent, arrived, where):
        return send(ref, ref, sent, arrived, where)

    barrier = pltpu.get_barrier_semaphore()
    for s in reversed(range(1, ne)):
        signal({"entity": ahead(s)})
    loads = [
        pltpu.make_async_copy(src, dst, lsem.at[k])
        for k, (src, dst) in enumerate([
            (req_hbm, req_v), (table_hbm, table), (head_hbm, head_v), (tail_hbm, tail_v),
            (neg_hbm, neg_v), (rel_hbm, rel_v), (panel_hbm, panel),
        ])
    ]
    for load in loads:
        load.start()
    for i in far_first:
        signal({"bucket": bucket_peer(i)})

    loads[0].wait()
    req = req_v[...]
    repeat = (iota((cap, slots), 0) == lax.rem(iota((cap, slots), 1), cap)).astype(F32).astype(BF)
    high = mm((req >> 5).astype(F32).astype(BF), repeat)
    low = mm((req & 31).astype(F32).astype(BF), repeat)
    wide[...] = (high * 32.0 + low).astype(jnp.int32)
    for s in range(ne):
        mine = iota((1, slots), 1) // cap == s
        msg[s] = jnp.where(mine, wide[pl.ds(ahead(s), 1), :], 0)

    pl.semaphore_wait(barrier, ne + nb - 2)

    for s in reversed(range(1, ne)):
        send(msg.at[s], reqbuf.at[s], ask_sem.at[0], ask_sem.at[1], {"entity": ahead(s)}).start()
    loads[1].wait()
    asks = whole(reqbuf.at[1:ne], ask_sem.at[0], ask_sem.at[1], {"entity": ahead(1)})
    asks.wait_recv()
    asked = msg[0]
    for s in range(1, ne):
        asked = asked + reqbuf[s]
    asked_all[0] = asked

    asked_col = to_col(asked.astype(F32)).astype(jnp.int32)
    pick = (iota((slots, table_rows), 1) == asked_col).astype(F32).astype(BF)
    rows[...] = mm(pick, table[...]).astype(BF)

    def at_slot(s):
        return slice(s * cap, (s + 1) * cap)

    def at_entity(o):
        return pl.ds(pl.multiple_of(o * cap, cap), cap)

    for s in reversed(range(1, ne)):
        send(rows.at[at_slot(s)], fetched.at[at_entity(e)], row_sem.at[0], row_sem.at[1],
             {"entity": behind(s)}).start()
    for i in far_first:
        send(asked_all.at[0], asked_all.at[i], list_sem.at[0], list_sem.at[1],
             {"bucket": bucket_peer(i)}).start()
    asks.wait_send()
    fetched[at_entity(e), :] = rows[at_slot(0), :]

    for load in loads[2:]:
        load.wait()
    tables = slot_tables(head_v, tail_v, neg_v, count_ref[0], slots)
    returns = whole(rows.at[cap:], row_sem.at[0], row_sem.at[1], {"entity": ahead(1)})
    returns.wait_recv()

    grad_proj, grad_rel = local_terms(fetched[...], panel[...], rel_v[...].astype(F32), tables)
    gf[...] = mm(grad_proj, panel[...]).astype(BF)

    for h in range(HALVES):
        for s in reversed(range(max(h * per_half, 1), (h + 1) * per_half)):
            send(gf.at[at_entity(ahead(s))], grecv.at[at_slot(s)], grad_sem.at[0],
                 grad_sem.at[1 + h], {"entity": ahead(s)}).start()
    grecv[at_slot(0), :] = gf[at_entity(e), :]
    rel_out[...] = grad_rel
    proj_out[...] = grad_proj
    fetched_out[...] = fetched[...]

    returns.wait_send()

    near_first = [0] + far_first[::-1]
    group = nb // GROUPS
    for h in range(HALVES):
        first = max(h * half_lanes, cap)
        last = (h + 1) * half_lanes
        whole(grecv.at[first:last], grad_sem.at[0], grad_sem.at[1 + h],
              {"entity": ahead(1)}).wait_recv()
        piece = grecv[h * half_lanes : last, :].astype(F32)
        gt[h] = piece.T.astype(BF)
        for p in reversed(range(1, nb)):
            peer = bucket_peer(near_first[p])
            send(gt.at[h, pl.ds(pl.multiple_of(peer * width, width), width), :],
                 frecv.at[h, p], part_sem.at[0], part_sem.at[1 + h * GROUPS + p // group],
                 {"bucket": peer}).start()
        frecv[h, 0] = gt[h, pl.ds(pl.multiple_of(b * width, width), width), :]
        if h == 0:
            lists = whole(asked_all.at[1:nb], list_sem.at[0], list_sem.at[1],
                          {"bucket": bucket_peer(1)})
            lists.wait()
            for p in range(nb):
                for k in range(HALVES):
                    hi = asked_all[near_first[p], :, k * half_lanes : (k + 1) * half_lanes]
                    hot[k, :, p * half_lanes : (p + 1) * half_lanes] = one_hot(
                        hi & (LANES - 1), LANES).astype(BF)

    total = None
    for h in range(HALVES):
        for q in range(GROUPS):
            first = max(q * group, 1)
            whole(frecv.at[h, first : (q + 1) * group], part_sem.at[0],
                  part_sem.at[1 + h * GROUPS + q], {"bucket": bucket_peer(1)}).wait_recv()
            for p in range(q * group, (q + 1) * group):
                lo = asked_all[near_first[p], :, h * half_lanes : (h + 1) * half_lanes] >> 7
                g = frecv[h, p].astype(F32)
                spread[h, :, p * half_lanes : (p + 1) * half_lanes] = jnp.concatenate(
                    [jnp.where(lo == k, g, 0.0) for k in range(high_rows)], axis=0).astype(BF)
        share = mm_nt(spread[h], hot[h])
        total = share if total is None else total + share
    whole(grecv.at[cap:], grad_sem.at[0], grad_sem.at[1], {"entity": ahead(1)}).wait_send()
    for h in range(HALVES):
        whole(frecv.at[h, 1:nb], part_sem.at[0], part_sem.at[1],
              {"bucket": bucket_peer(1)}).wait_send()
    for k in range(high_rows):
        ent_ref[:, k * LANES : (k + 1) * LANES] = total[k * width : (k + 1) * width, :]


def finish(ent_ref, proj_ref, fetched_ref, rel_ref, ent_out, panel_out, rel_out, held, sem):
    outs = [
        pltpu.make_async_copy(ent_ref, ent_out, sem.at[0]),
        pltpu.make_async_copy(rel_ref, rel_out, sem.at[1]),
    ]
    for out in outs:
        out.start()
    half = held.shape[0] // 2
    for h in range(2):
        part = slice(h * half, (h + 1) * half)
        held[part, :] = mm_tn(proj_ref[:, part], fetched_ref[...])
        out = pltpu.make_async_copy(held.at[part], panel_out.at[part], sem.at[2 + h])
        out.start()
        outs.append(out)
    for out in outs:
        out.wait()


def body(ent_table, panels, rel_vecs, head_slots, tail_slots, negatives, requests, block_count):
    nb = lax.axis_size("bucket")
    ne = lax.axis_size("entity")
    rows, feat = ent_table.shape
    cap = requests.shape[2]
    slots = ne * cap
    width = feat // nb
    half = slots // HALVES
    vmem = pl.BlockSpec(memory_space=pltpu.VMEM)
    hbm = pl.BlockSpec(memory_space=pltpu.HBM)
    dma = pltpu.SemaphoreType.DMA
    shapes = (
        jax.ShapeDtypeStruct((width, rows), F32),
        jax.ShapeDtypeStruct((slots, feat), BF),
        jax.ShapeDtypeStruct((slots, feat), BF),
        jax.ShapeDtypeStruct((1, feat), F32),
    )
    ent_t, grad_proj, fetched, grad_rel = pl.pallas_call(
        functools.partial(kernel, nb, ne),
        out_shape=shapes,
        in_specs=[hbm] * 7 + [pl.BlockSpec(memory_space=pltpu.SMEM)],
        out_specs=(vmem,) * 4,
        scratch_shapes=[
            pltpu.VMEM((rows, feat), BF),
            pltpu.VMEM((feat, feat), BF),
            pltpu.VMEM(rel_vecs.shape, BF),
            pltpu.VMEM(head_slots.shape[1:], jnp.int32),
            pltpu.VMEM(tail_slots.shape[1:], jnp.int32),
            pltpu.VMEM(negatives.shape[1:], jnp.int32),
            pltpu.VMEM(requests.shape[1:], jnp.int32),
            pltpu.VMEM((ne, slots), jnp.int32),
            pltpu.VMEM((ne, 1, slots), jnp.int32),
            pltpu.VMEM((ne, 1, slots), jnp.int32),
            pltpu.VMEM((nb, 1, slots), jnp.int32),
            pltpu.VMEM((slots, feat), BF),
            pltpu.VMEM((slots, feat), BF),
            pltpu.VMEM((slots, feat), BF),
            pltpu.VMEM((slots, feat), BF),
            pltpu.VMEM((HALVES, feat, half), BF),
            pltpu.VMEM((HALVES, nb, width, half), BF),
            pltpu.VMEM((HALVES, rows // LANES * width, nb * half), BF),
            pltpu.VMEM((HALVES, LANES, nb * half), BF),
            dma((7,)),
            dma((2,)),
            dma((2,)),
            dma((2,)),
            dma((1 + HALVES,)),
            dma((1 + HALVES * GROUPS,)),
        ],
        compiler_params=pltpu.CompilerParams(
            collective_id=0, has_side_effects=True, vmem_limit_bytes=40 * 1024 * 1024
        ),
        name="transr",
    )(
        *(pltpu.with_memory_space_constraint(x, pltpu.HBM) for x in (
            ent_table, panels[0], rel_vecs, head_slots[0], tail_slots[0], negatives[0],
            requests[0])),
        block_count,
    )
    ent_t, grad_panel, grad_rel = pl.pallas_call(
        finish,
        out_shape=(shapes[0], jax.ShapeDtypeStruct((feat, feat), F32), shapes[3]),
        in_specs=[vmem] * 4,
        out_specs=(hbm,) * 3,
        scratch_shapes=[pltpu.VMEM((feat, feat), F32), dma((4,))],
        compiler_params=pltpu.CompilerParams(vmem_limit_bytes=8 * 1024 * 1024),
        name="finish",
    )(ent_t, grad_proj, fetched, grad_rel)
    return (ent_t.T, grad_panel[None], grad_rel)


def solution(mesh):
    both = ("bucket", "entity")
    placed = (
        P("entity", None),
        P(both, None, None),
        P(both, None),
        P(both, None, None),
        P(both, None, None),
        P(both, None, None),
        P(both, None, None),
        P(both),
    )
    return jax.shard_map(
        body,
        mesh=mesh,
        in_specs=placed,
        out_specs=(P("entity", "bucket"), P(both, None, None), P(both, None)),
        check_vma=False,
    )
```

```python
import functools

import jax
import jax.numpy as jnp
from jax import lax
from jax.experimental import pallas as pl
from jax.experimental.pallas import tpu as pltpu
from jax.sharding import PartitionSpec as P

MARGIN = 2.0
LANES = 128
HALVES = 2
GROUPS = 4
X_SIZE = 4
MESH = pl.DeviceIdType.MESH
BF = jnp.bfloat16
F32 = jnp.float32


def mm(a, b):
    return jnp.dot(a, b, preferred_element_type=F32)


def mm_nt(a, b):
    return lax.dot_general(a, b, (((1,), (1,)), ((), ())), preferred_element_type=F32)


def mm_tn(a, b):
    return lax.dot_general(a, b, (((0,), (0,)), ((), ())), preferred_element_type=F32)


def iota(shape, axis):
    return lax.broadcasted_iota(jnp.int32, shape, axis)


def to_col(row):
    n = row.shape[1]
    eye = iota((n, n), 0) == iota((n, n), 1)
    return jnp.sum(jnp.where(eye, row, 0.0), axis=1, keepdims=True)


def to_row(col):
    n = col.shape[0]
    eye = iota((n, n), 0) == iota((n, n), 1)
    return jnp.sum(jnp.where(eye, col, 0.0), axis=0, keepdims=True)


def one_hot(row, n):
    return (iota((n, row.shape[1]), 0) == row).astype(F32)


def slot_tables(head_ref, tail_ref, neg_ref, live_count, slots):
    blocks, edge = head_ref.shape
    edges = blocks * edge
    head = jnp.concatenate([head_ref[j : j + 1, :] for j in range(blocks)], axis=1)
    tail = jnp.concatenate([tail_ref[j : j + 1, :] for j in range(blocks)], axis=1)
    head_t = one_hot(head, slots)
    tail_t = one_hot(tail, slots)
    block_of = iota((edges, 1), 0) // edge
    live = (block_of < live_count).astype(F32)
    count = jnp.zeros((edges, slots), F32)
    for j in range(blocks):
        hits = jnp.sum(one_hot(neg_ref[j : j + 1, :], slots), axis=1, keepdims=True)
        count = jnp.where(block_of == j, to_row(hits), count)
    count = count * (live * (1.0 / neg_ref.shape[1]))
    return head_t.astype(BF), tail_t.astype(BF), head_t.T.astype(BF), tail_t.T.astype(BF), live, count


def local_terms(fetched, panel, rel, tables):
    head_t, tail_t, head, tail, live, count = tables
    proj = mm_nt(fetched, panel).astype(BF)
    proj_f = proj.astype(F32)
    centers = (mm(head, proj) + rel).astype(BF)
    center_f = centers.astype(F32)
    offset = center_f - mm(tail, proj)
    pos_weight = jax.nn.sigmoid(jnp.sum(offset * offset, axis=1, keepdims=True) - MARGIN) * live
    proj_sq = to_row(jnp.sum(proj_f * proj_f, axis=1, keepdims=True))
    center_sq = jnp.sum(center_f * center_f, axis=1, keepdims=True)
    dist = center_sq + proj_sq - 2.0 * mm_nt(centers, proj)
    weight = -jax.nn.sigmoid(MARGIN - dist) * count
    weight_t = weight.T
    pulled = 2.0 * pos_weight * offset
    grad_center = (
        pulled
        + 2.0 * jnp.sum(weight, axis=1, keepdims=True) * center_f
        - 2.0 * mm(weight.astype(BF), proj)
    )
    grad_proj = (
        mm(head_t, grad_center.astype(BF))
        - mm(tail_t, pulled.astype(BF))
        + 2.0 * jnp.sum(weight_t, axis=1, keepdims=True) * proj_f
        - 2.0 * mm(weight_t.astype(BF), centers)
    ).astype(BF)
    return grad_proj, jnp.sum(grad_center, axis=0, keepdims=True)


def away(step, size):
    return min(step, size - step)


def kernel(
    nb, ne,
    table_hbm, panel_hbm, rel_hbm, head_hbm, tail_hbm, neg_hbm, req_hbm, count_ref,
    ent_ref, panel_out, rel_out,
    table, panel, rel_v, head_v, tail_v, neg_v, req_v, wide,
    msg, reqbuf, asked_all, rows, fetched, gf, grecv, gt, frecv, spread, hot,
    lsem, ask_sem, list_sem, row_sem, grad_sem, part_sem,
):
    b = lax.axis_index("bucket")
    e = lax.axis_index("entity")
    cap = req_v.shape[1]
    slots = ne * cap
    width = frecv.shape[2]
    per_half = ne // HALVES
    half_lanes = per_half * cap
    table_rows = table.shape[0]
    high_rows = table_rows // LANES

    chips = ne // 2
    steps = sorted(range(chips), key=lambda d: away(d, chips))

    def ahead(s):
        return 2 * ((e // 2 + steps[s // 2]) & (chips - 1)) + ((e + s) & 1)

    def behind(s):
        return 2 * ((e // 2 - steps[s // 2]) & (chips - 1)) + ((e + s) & 1)

    zs = nb // X_SIZE
    mine = lax.rem(b, zs) * X_SIZE + b // zs

    def others(do):
        def step(q, carry):
            @pl.when(q != mine)
            def _():
                do({"bucket": lax.rem(q, X_SIZE) * zs + q // X_SIZE})

            return carry

        lax.fori_loop(0, nb, step, 0)

    some_bucket = {"bucket": lax.rem(b + 1, nb)}
    some_entity = {"entity": lax.rem(e + 1, ne)}

    def signal(where):
        pl.semaphore_signal(barrier, inc=1, device_id=where, device_id_type=MESH)

    def send(src, dst, sent, arrived, where):
        return pltpu.make_async_remote_copy(
            src_ref=src, dst_ref=dst, send_sem=sent, recv_sem=arrived,
            device_id=where, device_id_type=MESH)

    def whole(ref, sent, arrived, where):
        return send(ref, ref, sent, arrived, where)

    barrier = pltpu.get_barrier_semaphore()
    for s in reversed(range(1, ne)):
        signal({"entity": ahead(s)})
    loads = [
        pltpu.make_async_copy(src, dst, lsem.at[k])
        for k, (src, dst) in enumerate([
            (req_hbm, req_v), (table_hbm, table), (head_hbm, head_v), (tail_hbm, tail_v),
            (neg_hbm, neg_v), (rel_hbm, rel_v), (panel_hbm, panel),
        ])
    ]
    for load in loads:
        load.start()
    others(signal)

    loads[0].wait()
    req = req_v[...]
    repeat = (iota((cap, half_lanes), 0) == lax.rem(iota((cap, half_lanes), 1), cap)).astype(F32).astype(BF)
    high = mm((req >> 5).astype(F32).astype(BF), repeat)
    low = mm((req & 31).astype(F32).astype(BF), repeat)
    wide[...] = (high * 32.0 + low).astype(jnp.int32)
    for s in range(ne):
        here = iota((1, half_lanes), 1) // cap == s % per_half
        msg[s] = jnp.where(here, wide[pl.ds(ahead(s), 1), :], 0)

    pl.semaphore_wait(barrier, ne + nb - 2)

    for s in reversed(range(1, ne)):
        send(msg.at[s], reqbuf.at[s], ask_sem.at[0], ask_sem.at[1 + s // per_half],
             {"entity": ahead(s)}).start()

    def at_slot(s):
        return slice(s * cap, (s + 1) * cap)

    def at_entity(o):
        return pl.ds(pl.multiple_of(o * cap, cap), cap)

    loads[1].wait()
    for h in range(HALVES):
        first = max(h * per_half, 1)
        last = (h + 1) * per_half
        whole(reqbuf.at[first:last], ask_sem.at[0], ask_sem.at[1 + h], some_entity).wait_recv()
        asked = reqbuf[first] + (reqbuf[first + 1] if h else msg[0])
        for s in range(first + 1 + h, last):
            asked = asked + reqbuf[s]
        asked_all[mine, :, h * half_lanes : last * cap] = asked
        asked_col = to_col(asked.astype(F32)).astype(jnp.int32)
        pick = (iota((half_lanes, table_rows), 1) == asked_col).astype(F32).astype(BF)
        rows[h * half_lanes : last * cap, :] = mm(pick, table[...]).astype(BF)
        for s in reversed(range(first, last)):
            send(rows.at[at_slot(s)], fetched.at[at_entity(e)], row_sem.at[0], row_sem.at[1],
                 {"entity": behind(s)}).start()
    others(lambda peer: send(
        asked_all.at[mine], asked_all.at[mine], list_sem.at[0], list_sem.at[1], peer).start())
    whole(reqbuf.at[1:ne], ask_sem.at[0], ask_sem.at[1], some_entity).wait_send()
    fetched[at_entity(e), :] = rows[at_slot(0), :]

    for load in loads[2:]:
        load.wait()
    tables = slot_tables(head_v, tail_v, neg_v, count_ref[0], slots)
    returns = whole(rows.at[cap:], row_sem.at[0], row_sem.at[1], some_entity)
    returns.wait_recv()

    grad_proj, grad_rel = local_terms(fetched[...], panel[...], rel_v[...].astype(F32), tables)
    gf[...] = mm(grad_proj, panel[...]).astype(BF)

    for h in range(HALVES):
        for s in reversed(range(max(h * per_half, 1), (h + 1) * per_half)):
            send(gf.at[at_entity(ahead(s))], grecv.at[at_slot(s)], grad_sem.at[0],
                 grad_sem.at[1 + h], {"entity": ahead(s)}).start()
    grecv[at_slot(0), :] = gf[at_entity(e), :]
    rel_out[...] = grad_rel
    panel_out[...] = mm_tn(grad_proj, fetched[...])
    returns.wait_send()

    group = nb // GROUPS
    my_group = mine // group
    my_columns = pl.ds(pl.multiple_of(b * width, width), width)
    for h in range(HALVES):
        first = max(h * half_lanes, cap)
        last = (h + 1) * half_lanes
        whole(grecv.at[first:last], grad_sem.at[0], grad_sem.at[1 + h], some_entity).wait_recv()
        gt[h] = grecv[h * half_lanes : last, :].astype(F32).T.astype(BF)

        def part(peer, h=h):
            columns = pl.ds(pl.multiple_of(peer["bucket"] * width, width), width)
            send(gt.at[h, columns, :], frecv.at[h, mine], part_sem.at[0],
                 part_sem.at[1 + h * GROUPS + my_group], peer).start()

        others(part)
        frecv[h, mine] = gt[h, my_columns, :]
        if h == 0:
            whole(asked_all.at[1:nb], list_sem.at[0], list_sem.at[1], some_bucket).wait()
            for q in range(nb):
                for k in range(HALVES):
                    hi = asked_all[q, :, k * half_lanes : (k + 1) * half_lanes] & (LANES - 1)
                    hot[k, :, q * half_lanes : (q + 1) * half_lanes] = one_hot(hi, LANES).astype(BF)

    total = None
    for h in range(HALVES):
        for k in range(GROUPS):
            def arrived(count, h=h, k=k):
                whole(frecv.at[h, k * group : k * group + count], part_sem.at[0],
                      part_sem.at[1 + h * GROUPS + k], some_bucket).wait_recv()

            pl.when(my_group == k)(lambda: arrived(group - 1))
            pl.when(my_group != k)(lambda: arrived(group))
            lanes = slice(k * group * half_lanes, (k + 1) * group * half_lanes)
            for q in range(k * group, (k + 1) * group):
                lo = asked_all[q, :, h * half_lanes : (h + 1) * half_lanes] >> 7
                g = frecv[h, q].astype(F32)
                spread[h, :, q * half_lanes : (q + 1) * half_lanes] = jnp.concatenate(
                    [jnp.where(lo == r, g, 0.0) for r in range(high_rows)], axis=0).astype(BF)
            share = mm_nt(spread[h, :, lanes], hot[h, :, lanes])
            total = share if total is None else total + share
    whole(grecv.at[cap:], grad_sem.at[0], grad_sem.at[1], some_entity).wait_send()
    for h in range(HALVES):
        whole(frecv.at[h, 1:nb], part_sem.at[0], part_sem.at[1], some_bucket).wait_send()
    for k in range(high_rows):
        ent_ref[:, k * LANES : (k + 1) * LANES] = total[k * width : (k + 1) * width, :]


def finish(ent_ref, panel_ref, rel_ref, ent_out, panel_out, rel_out, sem):
    outs = [
        pltpu.make_async_copy(src, dst, sem.at[k])
        for k, (src, dst) in enumerate([
            (panel_ref, panel_out), (ent_ref, ent_out), (rel_ref, rel_out)])
    ]
    for out in outs:
        out.start()
    for out in outs:
        out.wait()


def body(ent_table, panels, rel_vecs, head_slots, tail_slots, negatives, requests, block_count):
    nb = lax.axis_size("bucket")
    ne = lax.axis_size("entity")
    rows, feat = ent_table.shape
    cap = requests.shape[2]
    slots = ne * cap
    width = feat // nb
    half = slots // HALVES
    vmem = pl.BlockSpec(memory_space=pltpu.VMEM)
    hbm = pl.BlockSpec(memory_space=pltpu.HBM)
    dma = pltpu.SemaphoreType.DMA
    shapes = (
        jax.ShapeDtypeStruct((width, rows), F32),
        jax.ShapeDtypeStruct((feat, feat), F32),
        jax.ShapeDtypeStruct((1, feat), F32),
    )
    results = pl.pallas_call(
        functools.partial(kernel, nb, ne),
        out_shape=shapes,
        in_specs=[hbm] * 7 + [pl.BlockSpec(memory_space=pltpu.SMEM)],
        out_specs=(vmem,) * 3,
        scratch_shapes=[
            pltpu.VMEM((rows, feat), BF),
            pltpu.VMEM((feat, feat), BF),
            pltpu.VMEM(rel_vecs.shape, BF),
            pltpu.VMEM(head_slots.shape[1:], jnp.int32),
            pltpu.VMEM(tail_slots.shape[1:], jnp.int32),
            pltpu.VMEM(negatives.shape[1:], jnp.int32),
            pltpu.VMEM(requests.shape[1:], jnp.int32),
            pltpu.VMEM((ne, half), jnp.int32),
            pltpu.VMEM((ne, 1, half), jnp.int32),
            pltpu.VMEM((ne, 1, half), jnp.int32),
            pltpu.VMEM((nb, 1, slots), jnp.int32),
            pltpu.VMEM((slots, feat), BF),
            pltpu.VMEM((slots, feat), BF),
            pltpu.VMEM((slots, feat), BF),
            pltpu.VMEM((slots, feat), BF),
            pltpu.VMEM((HALVES, feat, half), BF),
            pltpu.VMEM((HALVES, nb, width, half), BF),
            pltpu.VMEM((HALVES, rows // LANES * width, nb * half), BF),
            pltpu.VMEM((HALVES, LANES, nb * half), BF),
            dma((7,)),
            dma((1 + HALVES,)),
            dma((2,)),
            dma((2,)),
            dma((1 + HALVES,)),
            dma((1 + HALVES * GROUPS,)),
        ],
        compiler_params=pltpu.CompilerParams(
            collective_id=0, has_side_effects=True, vmem_limit_bytes=40 * 1024 * 1024
        ),
        name="transr",
    )(
        *(pltpu.with_memory_space_constraint(x, pltpu.HBM) for x in (
            ent_table, panels[0], rel_vecs, head_slots[0], tail_slots[0], negatives[0],
            requests[0])),
        block_count,
    )
    ent_t, grad_panel, grad_rel = pl.pallas_call(
        finish,
        out_shape=shapes,
        in_specs=[vmem] * 3,
        out_specs=(hbm,) * 3,
        scratch_shapes=[dma((3,))],
        compiler_params=pltpu.CompilerParams(vmem_limit_bytes=8 * 1024 * 1024),
        name="finish",
    )(*results)
    return (ent_t.T, grad_panel[None], grad_rel)


def solution(mesh):
    both = ("bucket", "entity")
    placed = (
        P("entity", None),
        P(both, None, None),
        P(both, None),
        P(both, None, None),
        P(both, None, None),
        P(both, None, None),
        P(both, None, None),
        P(both),
    )
    return jax.shard_map(
        body,
        mesh=mesh,
        in_specs=placed,
        out_specs=(P("entity", "bucket"), P(both, None, None), P(both, None)),
        check_vma=False,
    )
```

```python
import functools

import jax
import jax.numpy as jnp
from jax import lax
from jax.experimental import pallas as pl
from jax.experimental.pallas import tpu as pltpu
from jax.sharding import PartitionSpec as P

MARGIN = 2.0
LANES = 128
HALVES = 2
GROUPS = 4
CUTS = (0, 2, 8)
X_SIZE = 4
MESH = pl.DeviceIdType.MESH
BF = jnp.bfloat16
F32 = jnp.float32


def mm(a, b):
    return jnp.dot(a, b, preferred_element_type=F32)


def mm_nt(a, b):
    return lax.dot_general(a, b, (((1,), (1,)), ((), ())), preferred_element_type=F32)


def mm_tn(a, b):
    return lax.dot_general(a, b, (((0,), (0,)), ((), ())), preferred_element_type=F32)


def iota(shape, axis):
    return lax.broadcasted_iota(jnp.int32, shape, axis)


def to_col(row):
    n = row.shape[1]
    eye = iota((n, n), 0) == iota((n, n), 1)
    return jnp.sum(jnp.where(eye, row, 0.0), axis=1, keepdims=True)


def to_row(col):
    n = col.shape[0]
    eye = iota((n, n), 0) == iota((n, n), 1)
    return jnp.sum(jnp.where(eye, col, 0.0), axis=0, keepdims=True)


def one_hot(row, n):
    return (iota((n, row.shape[1]), 0) == row).astype(F32)


def slot_tables(head_ref, tail_ref, neg_ref, live_count, slots):
    blocks, edge = head_ref.shape
    edges = blocks * edge
    head = jnp.concatenate([head_ref[j : j + 1, :] for j in range(blocks)], axis=1)
    tail = jnp.concatenate([tail_ref[j : j + 1, :] for j in range(blocks)], axis=1)
    head_t = one_hot(head, slots)
    tail_t = one_hot(tail, slots)
    block_of = iota((edges, 1), 0) // edge
    live = (block_of < live_count).astype(F32)
    count = jnp.zeros((edges, slots), F32)
    for j in range(blocks):
        hits = jnp.sum(one_hot(neg_ref[j : j + 1, :], slots), axis=1, keepdims=True)
        count = jnp.where(block_of == j, to_row(hits), count)
    count = count * (live * (1.0 / neg_ref.shape[1]))
    return head_t.astype(BF), tail_t.astype(BF), head_t.T.astype(BF), tail_t.T.astype(BF), live, count


def local_terms(fetched, panel, rel, tables):
    head_t, tail_t, head, tail, live, count = tables
    proj = mm_nt(fetched, panel).astype(BF)
    proj_f = proj.astype(F32)
    centers = (mm(head, proj) + rel).astype(BF)
    center_f = centers.astype(F32)
    offset = center_f - mm(tail, proj)
    pos_weight = jax.nn.sigmoid(jnp.sum(offset * offset, axis=1, keepdims=True) - MARGIN) * live
    proj_sq = to_row(jnp.sum(proj_f * proj_f, axis=1, keepdims=True))
    center_sq = jnp.sum(center_f * center_f, axis=1, keepdims=True)
    dist = center_sq + proj_sq - 2.0 * mm_nt(centers, proj)
    weight = -jax.nn.sigmoid(MARGIN - dist) * count
    weight_t = weight.T
    pulled = 2.0 * pos_weight * offset
    grad_center = (
        pulled
        + 2.0 * jnp.sum(weight, axis=1, keepdims=True) * center_f
        - 2.0 * mm(weight.astype(BF), proj)
    )
    grad_proj = (
        mm(head_t, grad_center.astype(BF))
        - mm(tail_t, pulled.astype(BF))
        + 2.0 * jnp.sum(weight_t, axis=1, keepdims=True) * proj_f
        - 2.0 * mm(weight_t.astype(BF), centers)
    ).astype(BF)
    return grad_proj, jnp.sum(grad_center, axis=0, keepdims=True)


def away(step, size):
    return min(step, size - step)


def kernel(
    nb, ne,
    table_hbm, panel_hbm, rel_hbm, head_hbm, tail_hbm, neg_hbm, req_hbm, count_ref,
    ent_ref, panel_out, rel_out,
    table, panel, panel_q, rel_v, head_v, tail_v, neg_v, req_v, wide,
    msg, reqbuf, asked_all, rows, fetched, gf, grecv, gt, frecv, spread, hot,
    lsem, ask_sem, list_sem, row_sem, grad_sem, part_sem,
):
    b = lax.axis_index("bucket")
    e = lax.axis_index("entity")
    cap = req_v.shape[1]
    slots = ne * cap
    width = frecv.shape[2]
    per_half = ne // HALVES
    half_lanes = per_half * cap
    table_rows = table.shape[0]
    high_rows = table_rows // LANES

    chips = ne // 2
    steps = sorted(range(chips), key=lambda d: away(d, chips))

    def ahead(s):
        return 2 * ((e // 2 + steps[s // 2]) & (chips - 1)) + ((e + s) & 1)

    def behind(s):
        return 2 * ((e // 2 - steps[s // 2]) & (chips - 1)) + ((e + s) & 1)

    zs = nb // X_SIZE
    mine = lax.rem(b, zs) * X_SIZE + b // zs

    far_first = sorted(
        range(1, nb), key=lambda i: -(away(i // zs, X_SIZE) + away(i % zs, zs)))

    def bucket_peer(i):
        return ((b // zs + i // zs) & (X_SIZE - 1)) * zs + ((b + i) & (zs - 1))

    def others(do):
        for q in range(nb):
            pl.when(q != mine)(functools.partial(do, q % X_SIZE * zs + q // X_SIZE))

    some_bucket = {"bucket": lax.rem(b + 1, nb)}
    some_entity = {"entity": lax.rem(e + 1, ne)}

    def signal(where):
        pl.semaphore_signal(barrier, inc=1, device_id=where, device_id_type=MESH)

    def send(src, dst, sent, arrived, where):
        return pltpu.make_async_remote_copy(
            src_ref=src, dst_ref=dst, send_sem=sent, recv_sem=arrived,
            device_id=where, device_id_type=MESH)

    def whole(ref, sent, arrived, where):
        return send(ref, ref, sent, arrived, where)

    loads = [
        pltpu.make_async_copy(src, dst, lsem.at[k])
        for k, (src, dst) in enumerate([
            (req_hbm, req_v), (table_hbm, table), (head_hbm, head_v), (tail_hbm, tail_v),
            (neg_hbm, neg_v), (rel_hbm, rel_v), (panel_hbm, panel),
        ])
    ]
    barrier = pltpu.get_barrier_semaphore()
    loads[0].start()
    for i in far_first:
        signal({"bucket": bucket_peer(i)})
    for s in reversed(range(1, ne)):
        signal({"entity": ahead(s)})
    for load in loads[1:]:
        load.start()

    loads[0].wait()
    req = req_v[...]
    repeat = (iota((cap, half_lanes), 0) == lax.rem(iota((cap, half_lanes), 1), cap)).astype(F32).astype(BF)
    high = mm((req >> 5).astype(F32).astype(BF), repeat)
    low = mm((req & 31).astype(F32).astype(BF), repeat)
    wide[...] = (high * 32.0 + low).astype(jnp.int32)
    for s in range(ne):
        here = iota((1, half_lanes), 1) // cap == s % per_half
        msg[s] = jnp.where(here, wide[pl.ds(ahead(s), 1), :], 0)

    pl.semaphore_wait(barrier, ne + nb - 2)

    for s in reversed(range(1, ne)):
        send(msg.at[s], reqbuf.at[s], ask_sem.at[0], ask_sem.at[1 + s // per_half],
             {"entity": ahead(s)}).start()

    def at_slot(s):
        return slice(s * cap, (s + 1) * cap)

    def at_entity(o):
        return pl.ds(pl.multiple_of(o * cap, cap), cap)

    loads[1].wait()
    for h in range(HALVES):
        first = max(h * per_half, 1)
        last = (h + 1) * per_half
        whole(reqbuf.at[first:last], ask_sem.at[0], ask_sem.at[1 + h], some_entity).wait_recv()
        asked = reqbuf[first] + (reqbuf[first + 1] if h else msg[0])
        for s in range(first + 1 + h, last):
            asked = asked + reqbuf[s]
        asked_all[mine, :, h * half_lanes : last * cap] = asked
        asked_col = to_col(asked.astype(F32)).astype(jnp.int32)
        pick = (iota((half_lanes, table_rows), 1) == asked_col).astype(F32).astype(BF)
        rows[h * half_lanes : last * cap, :] = mm(pick, table[...]).astype(BF)
        for s in reversed(range(first, last)):
            send(rows.at[at_slot(s)], fetched.at[at_entity(e)], row_sem.at[0], row_sem.at[1],
                 {"entity": behind(s)}).start()
    others(lambda peer: send(
        asked_all.at[mine], asked_all.at[mine], list_sem.at[0], list_sem.at[1],
        {"bucket": peer}).start())
    whole(reqbuf.at[1:ne], ask_sem.at[0], ask_sem.at[1], some_entity).wait_send()
    fetched[at_entity(e), :] = rows[at_slot(0), :]

    for load in loads[2:]:
        load.wait()
    feat = panel.shape[1]
    at = iota((feat, feat), 1)
    q_of = at // width
    source = (lax.rem(q_of, X_SIZE) * zs + q_of // X_SIZE) * width + lax.rem(at, width)
    order = (iota((feat, feat), 0) == source).astype(F32).astype(BF)
    panel_q[...] = mm(panel[...], order).astype(BF)
    tables = slot_tables(head_v, tail_v, neg_v, count_ref[0], slots)
    returns = whole(rows.at[cap:], row_sem.at[0], row_sem.at[1], some_entity)
    returns.wait_recv()

    grad_proj, grad_rel = local_terms(fetched[...], panel[...], rel_v[...].astype(F32), tables)
    gf[...] = mm(grad_proj, panel_q[...]).astype(BF)

    pieces = [(cut, h) for cut in zip(CUTS, CUTS[1:]) for h in range(HALVES)]
    for n, (cut, h) in enumerate(pieces):
        columns = slice(cut[0] * nb // 8 * width, cut[1] * nb // 8 * width)
        for s in reversed(range(max(h * per_half, 1), (h + 1) * per_half)):
            send(gf.at[at_entity(ahead(s)), columns], grecv.at[at_slot(s), columns],
                 grad_sem.at[0], grad_sem.at[1 + n], {"entity": ahead(s)}).start()
    grecv[at_slot(0), :] = gf[at_entity(e), :]
    rel_out[...] = grad_rel
    panel_out[...] = mm_tn(grad_proj, fetched[...])
    returns.wait_send()

    group = nb // GROUPS
    my_group = mine // group
    my_columns = pl.ds(pl.multiple_of(mine * width, width), width)
    def part(h, q):
        peer = q % X_SIZE * zs + q // X_SIZE
        send(gt.at[h, q * width : (q + 1) * width, :], frecv.at[h, mine], part_sem.at[0],
             part_sem.at[1 + h * GROUPS + my_group], {"bucket": peer}).start()

    for n, (cut, h) in enumerate(pieces):
        columns = slice(cut[0] * nb // 8 * width, cut[1] * nb // 8 * width)
        first = max(h * half_lanes, cap)
        last = (h + 1) * half_lanes
        whole(grecv.at[first:last, columns], grad_sem.at[0], grad_sem.at[1 + n],
              some_entity).wait_recv()
        gt[h, columns, :] = grecv[h * half_lanes : last, columns].astype(F32).T.astype(BF)
        for q in range(cut[0] * nb // 8, cut[1] * nb // 8):
            pl.when(q != mine)(functools.partial(part, h, q))
        if cut[1] == CUTS[-1]:
            frecv[h, mine] = gt[h, my_columns, :]
        if n == 0:
            whole(asked_all.at[1:nb], list_sem.at[0], list_sem.at[1], some_bucket).wait()
            for q in range(nb):
                for k in range(HALVES):
                    hi = asked_all[q, :, k * half_lanes : (k + 1) * half_lanes] & (LANES - 1)
                    hot[k, :, q * half_lanes : (q + 1) * half_lanes] = one_hot(hi, LANES).astype(BF)

    total = None
    for h in range(HALVES):
        for k in range(GROUPS):
            def arrived(count, h=h, k=k):
                whole(frecv.at[h, k * group : k * group + count], part_sem.at[0],
                      part_sem.at[1 + h * GROUPS + k], some_bucket).wait_recv()

            pl.when(my_group == k)(lambda: arrived(group - 1))
            pl.when(my_group != k)(lambda: arrived(group))
            lanes = slice(k * group * half_lanes, (k + 1) * group * half_lanes)
            for q in range(k * group, (k + 1) * group):
                lo = asked_all[q, :, h * half_lanes : (h + 1) * half_lanes] >> 7
                g = frecv[h, q].astype(F32)
                spread[h, :, q * half_lanes : (q + 1) * half_lanes] = jnp.concatenate(
                    [jnp.where(lo == r, g, 0.0) for r in range(high_rows)], axis=0).astype(BF)
            share = mm_nt(spread[h, :, lanes], hot[h, :, lanes])
            total = share if total is None else total + share
    whole(grecv.at[cap:], grad_sem.at[0], grad_sem.at[1], some_entity).wait_send()
    for h in range(HALVES):
        whole(frecv.at[h, 1:nb], part_sem.at[0], part_sem.at[1], some_bucket).wait_send()
    for k in range(high_rows):
        ent_ref[:, k * LANES : (k + 1) * LANES] = total[k * width : (k + 1) * width, :]


def finish(ent_ref, panel_ref, rel_ref, ent_out, panel_out, rel_out, sem):
    outs = [
        pltpu.make_async_copy(src, dst, sem.at[k])
        for k, (src, dst) in enumerate([
            (panel_ref, panel_out), (ent_ref, ent_out), (rel_ref, rel_out)])
    ]
    for out in outs:
        out.start()
    for out in outs:
        out.wait()


def body(ent_table, panels, rel_vecs, head_slots, tail_slots, negatives, requests, block_count):
    nb = lax.axis_size("bucket")
    ne = lax.axis_size("entity")
    rows, feat = ent_table.shape
    cap = requests.shape[2]
    slots = ne * cap
    width = feat // nb
    half = slots // HALVES
    vmem = pl.BlockSpec(memory_space=pltpu.VMEM)
    hbm = pl.BlockSpec(memory_space=pltpu.HBM)
    dma = pltpu.SemaphoreType.DMA
    shapes = (
        jax.ShapeDtypeStruct((width, rows), F32),
        jax.ShapeDtypeStruct((feat, feat), F32),
        jax.ShapeDtypeStruct((1, feat), F32),
    )
    results = pl.pallas_call(
        functools.partial(kernel, nb, ne),
        out_shape=shapes,
        in_specs=[hbm] * 7 + [pl.BlockSpec(memory_space=pltpu.SMEM)],
        out_specs=(vmem,) * 3,
        scratch_shapes=[
            pltpu.VMEM((rows, feat), BF),
            pltpu.VMEM((feat, feat), BF),
            pltpu.VMEM((feat, feat), BF),
            pltpu.VMEM(rel_vecs.shape, BF),
            pltpu.VMEM(head_slots.shape[1:], jnp.int32),
            pltpu.VMEM(tail_slots.shape[1:], jnp.int32),
            pltpu.VMEM(negatives.shape[1:], jnp.int32),
            pltpu.VMEM(requests.shape[1:], jnp.int32),
            pltpu.VMEM((ne, half), jnp.int32),
            pltpu.VMEM((ne, 1, half), jnp.int32),
            pltpu.VMEM((ne, 1, half), jnp.int32),
            pltpu.VMEM((nb, 1, slots), jnp.int32),
            pltpu.VMEM((slots, feat), BF),
            pltpu.VMEM((slots, feat), BF),
            pltpu.VMEM((slots, feat), BF),
            pltpu.VMEM((slots, feat), BF),
            pltpu.VMEM((HALVES, feat, half), BF),
            pltpu.VMEM((HALVES, nb, width, half), BF),
            pltpu.VMEM((HALVES, rows // LANES * width, nb * half), BF),
            pltpu.VMEM((HALVES, LANES, nb * half), BF),
            dma((7,)),
            dma((1 + HALVES,)),
            dma((2,)),
            dma((2,)),
            dma((1 + HALVES * (len(CUTS) - 1),)),
            dma((1 + HALVES * GROUPS,)),
        ],
        compiler_params=pltpu.CompilerParams(
            collective_id=0, has_side_effects=True, vmem_limit_bytes=40 * 1024 * 1024
        ),
        name="transr",
    )(
        *(pltpu.with_memory_space_constraint(x, pltpu.HBM) for x in (
            ent_table, panels[0], rel_vecs, head_slots[0], tail_slots[0], negatives[0],
            requests[0])),
        block_count,
    )
    ent_t, grad_panel, grad_rel = pl.pallas_call(
        finish,
        out_shape=shapes,
        in_specs=[vmem] * 3,
        out_specs=(hbm,) * 3,
        scratch_shapes=[dma((3,))],
        compiler_params=pltpu.CompilerParams(vmem_limit_bytes=8 * 1024 * 1024),
        name="finish",
    )(*results)
    return (ent_t.T, grad_panel[None], grad_rel)


def solution(mesh):
    both = ("bucket", "entity")
    placed = (
        P("entity", None),
        P(both, None, None),
        P(both, None),
        P(both, None, None),
        P(both, None, None),
        P(both, None, None),
        P(both, None, None),
        P(both),
    )
    return jax.shard_map(
        body,
        mesh=mesh,
        in_specs=placed,
        out_specs=(P("entity", "bucket"), P(both, None, None), P(both, None)),
        check_vma=False,
    )
```

```python
import functools

import jax
import jax.numpy as jnp
from jax import lax
from jax.experimental import pallas as pl
from jax.experimental.pallas import tpu as pltpu
from jax.sharding import PartitionSpec as P

MARGIN = 2.0
LANES = 128
HALVES = 2
GROUPS = 4
CUTS = (0, 2, 8)
X_SIZE = 4
MESH = pl.DeviceIdType.MESH
BF = jnp.bfloat16
F32 = jnp.float32


def mm(a, b):
    return jnp.dot(a, b, preferred_element_type=F32)


def mm_nt(a, b):
    return lax.dot_general(a, b, (((1,), (1,)), ((), ())), preferred_element_type=F32)


def mm_tn(a, b):
    return lax.dot_general(a, b, (((0,), (0,)), ((), ())), preferred_element_type=F32)


def iota(shape, axis):
    return lax.broadcasted_iota(jnp.int32, shape, axis)


def to_col(row):
    n = row.shape[1]
    eye = iota((n, n), 0) == iota((n, n), 1)
    return jnp.sum(jnp.where(eye, row, 0.0), axis=1, keepdims=True)


def to_row(col):
    n = col.shape[0]
    eye = iota((n, n), 0) == iota((n, n), 1)
    return jnp.sum(jnp.where(eye, col, 0.0), axis=0, keepdims=True)


def one_hot(row, n):
    return (iota((n, row.shape[1]), 0) == row).astype(F32)


def slot_tables(head_ref, tail_ref, neg_ref, live_count, slots):
    blocks, edge = head_ref.shape
    edges = blocks * edge
    head = jnp.concatenate([head_ref[j : j + 1, :] for j in range(blocks)], axis=1)
    tail = jnp.concatenate([tail_ref[j : j + 1, :] for j in range(blocks)], axis=1)
    head_t = one_hot(head, slots)
    tail_t = one_hot(tail, slots)
    block_of = iota((edges, 1), 0) // edge
    live = (block_of < live_count).astype(F32)
    count = jnp.zeros((edges, slots), F32)
    for j in range(blocks):
        hits = jnp.sum(one_hot(neg_ref[j : j + 1, :], slots), axis=1, keepdims=True)
        count = jnp.where(block_of == j, to_row(hits), count)
    count = count * (live * (1.0 / neg_ref.shape[1]))
    ends_t = jnp.concatenate([head_t, tail_t], axis=1)
    return ends_t.astype(BF), ends_t.T.astype(BF), live, count


def local_terms(fetched, panel, rel, tables):
    ends_t, ends, live, count = tables
    edges = live.shape[0]
    proj = mm_nt(fetched, panel).astype(BF)
    proj_f = proj.astype(F32)
    found = mm(ends, proj)
    centers = (found[:edges] + rel).astype(BF)
    center_f = centers.astype(F32)
    offset = center_f - found[edges:]
    pos_weight = jax.nn.sigmoid(jnp.sum(offset * offset, axis=1, keepdims=True) - MARGIN) * live
    proj_sq = to_row(jnp.sum(proj_f * proj_f, axis=1, keepdims=True))
    center_sq = jnp.sum(center_f * center_f, axis=1, keepdims=True)
    dist = center_sq + proj_sq - 2.0 * mm_nt(centers, proj)
    weight = -jax.nn.sigmoid(MARGIN - dist) * count
    weight_t = weight.T
    pulled = 2.0 * pos_weight * offset
    grad_center = (
        pulled
        + 2.0 * jnp.sum(weight, axis=1, keepdims=True) * center_f
        - 2.0 * mm(weight.astype(BF), proj)
    )
    onto = jnp.concatenate([ends_t, (-2.0 * weight_t).astype(BF)], axis=1)
    terms = jnp.concatenate([grad_center.astype(BF), (-pulled).astype(BF), centers], axis=0)
    grad_proj = mm(onto, terms) + 2.0 * jnp.sum(weight_t, axis=1, keepdims=True) * proj_f
    return grad_proj.astype(BF), jnp.sum(grad_center, axis=0, keepdims=True)


def away(step, size):
    return min(step, size - step)


def kernel(
    nb, ne,
    table_hbm, panel_hbm, rel_hbm, head_hbm, tail_hbm, neg_hbm, req_hbm, count_ref,
    ent_ref, panel_out, rel_out,
    table, panel, panel_q, rel_v, head_v, tail_v, neg_v, req_v, wide,
    msg, reqbuf, asked_all, rows, fetched, gf, grecv, gt, frecv, spread, hot,
    lsem, ask_sem, list_sem, row_sem, grad_sem, part_sem,
):
    b = lax.axis_index("bucket")
    e = lax.axis_index("entity")
    cap = req_v.shape[1]
    slots = ne * cap
    width = frecv.shape[2]
    per_half = ne // HALVES
    half_lanes = per_half * cap
    table_rows = table.shape[0]
    high_rows = table_rows // LANES

    chips = ne // 2
    steps = sorted(range(chips), key=lambda d: away(d, chips))

    def ahead(s):
        return 2 * ((e // 2 + steps[s // 2]) & (chips - 1)) + ((e + s) & 1)

    def behind(s):
        return 2 * ((e // 2 - steps[s // 2]) & (chips - 1)) + ((e + s) & 1)

    zs = nb // X_SIZE
    mine = lax.rem(b, zs) * X_SIZE + b // zs

    far_first = sorted(
        range(1, nb), key=lambda i: -(away(i // zs, X_SIZE) + away(i % zs, zs)))

    def bucket_peer(i):
        return ((b // zs + i // zs) & (X_SIZE - 1)) * zs + ((b + i) & (zs - 1))

    def others(do):
        for q in range(nb):
            pl.when(q != mine)(functools.partial(do, q % X_SIZE * zs + q // X_SIZE))

    some_bucket = {"bucket": lax.rem(b + 1, nb)}
    some_entity = {"entity": lax.rem(e + 1, ne)}

    def signal(where):
        pl.semaphore_signal(barrier, inc=1, device_id=where, device_id_type=MESH)

    def send(src, dst, sent, arrived, where):
        return pltpu.make_async_remote_copy(
            src_ref=src, dst_ref=dst, send_sem=sent, recv_sem=arrived,
            device_id=where, device_id_type=MESH)

    def whole(ref, sent, arrived, where):
        return send(ref, ref, sent, arrived, where)

    loads = [
        pltpu.make_async_copy(src, dst, lsem.at[k])
        for k, (src, dst) in enumerate([
            (req_hbm, req_v), (table_hbm, table), (head_hbm, head_v), (tail_hbm, tail_v),
            (neg_hbm, neg_v), (rel_hbm, rel_v), (panel_hbm, panel),
        ])
    ]
    barrier = pltpu.get_barrier_semaphore()
    loads[0].start()
    for i in far_first:
        signal({"bucket": bucket_peer(i)})
    for s in reversed(range(1, ne)):
        signal({"entity": ahead(s)})
    for load in loads[1:]:
        load.start()

    loads[0].wait()
    req = req_v[...]
    repeat = (iota((cap, half_lanes), 0) == lax.rem(iota((cap, half_lanes), 1), cap)).astype(F32).astype(BF)
    high = mm((req >> 5).astype(F32).astype(BF), repeat)
    low = mm((req & 31).astype(F32).astype(BF), repeat)
    wide[...] = (high * 32.0 + low).astype(jnp.int32)
    for s in range(ne):
        here = iota((1, half_lanes), 1) // cap == s % per_half
        msg[s] = jnp.where(here, wide[pl.ds(ahead(s), 1), :], 0)

    pl.semaphore_wait(barrier, ne + nb - 2)

    for s in reversed(range(1, ne)):
        send(msg.at[s], reqbuf.at[s], ask_sem.at[0], ask_sem.at[1 + s // per_half],
             {"entity": ahead(s)}).start()

    def at_slot(s):
        return slice(s * cap, (s + 1) * cap)

    def at_entity(o):
        return pl.ds(pl.multiple_of(o * cap, cap), cap)

    loads[1].wait()
    for h in range(HALVES):
        first = max(h * per_half, 1)
        last = (h + 1) * per_half
        whole(reqbuf.at[first:last], ask_sem.at[0], ask_sem.at[1 + h], some_entity).wait_recv()
        asked = reqbuf[first] + (reqbuf[first + 1] if h else msg[0])
        for s in range(first + 1 + h, last):
            asked = asked + reqbuf[s]
        asked_all[mine, :, h * half_lanes : last * cap] = asked
        asked_col = to_col(asked.astype(F32)).astype(jnp.int32)
        pick = (iota((half_lanes, table_rows), 1) == asked_col).astype(F32).astype(BF)
        rows[h * half_lanes : last * cap, :] = mm(pick, table[...]).astype(BF)
        for s in reversed(range(first, last)):
            send(rows.at[at_slot(s)], fetched.at[at_entity(e)], row_sem.at[0], row_sem.at[1],
                 {"entity": behind(s)}).start()
    others(lambda peer: send(
        asked_all.at[mine], asked_all.at[mine], list_sem.at[0], list_sem.at[1],
        {"bucket": peer}).start())
    whole(reqbuf.at[1:ne], ask_sem.at[0], ask_sem.at[1], some_entity).wait_send()
    fetched[at_entity(e), :] = rows[at_slot(0), :]

    for load in loads[2:]:
        load.wait()
    feat = panel.shape[1]
    at = iota((feat, feat), 1)
    q_of = at // width
    source = (lax.rem(q_of, X_SIZE) * zs + q_of // X_SIZE) * width + lax.rem(at, width)
    order = (iota((feat, feat), 0) == source).astype(F32).astype(BF)
    panel_q[...] = mm(panel[...], order).astype(BF)
    tables = slot_tables(head_v, tail_v, neg_v, count_ref[0], slots)
    returns = whole(rows.at[cap:], row_sem.at[0], row_sem.at[1], some_entity)
    returns.wait_recv()

    grad_proj, grad_rel = local_terms(fetched[...], panel[...], rel_v[...].astype(F32), tables)

    pieces = [(cut, h) for cut in zip(CUTS, CUTS[1:]) for h in range(HALVES)]
    for n, (cut, h) in enumerate(pieces):
        columns = slice(cut[0] * nb // 8 * width, cut[1] * nb // 8 * width)
        if h == 0:
            gf[:, columns] = mm(grad_proj, panel_q[:, columns]).astype(BF)
        for s in reversed(range(max(h * per_half, 1), (h + 1) * per_half)):
            send(gf.at[at_entity(ahead(s)), columns], grecv.at[at_slot(s), columns],
                 grad_sem.at[0], grad_sem.at[1 + n], {"entity": ahead(s)}).start()
    grecv[at_slot(0), :] = gf[at_entity(e), :]
    rel_out[...] = grad_rel
    returns.wait_send()

    group = nb // GROUPS
    my_group = mine // group
    my_columns = pl.ds(pl.multiple_of(mine * width, width), width)
    def part(h, q):
        peer = q % X_SIZE * zs + q // X_SIZE
        send(gt.at[h, q * width : (q + 1) * width, :], frecv.at[h, mine], part_sem.at[0],
             part_sem.at[1 + h * GROUPS + my_group], {"bucket": peer}).start()

    for n, (cut, h) in enumerate(pieces):
        columns = slice(cut[0] * nb // 8 * width, cut[1] * nb // 8 * width)
        first = max(h * half_lanes, cap)
        last = (h + 1) * half_lanes
        whole(grecv.at[first:last, columns], grad_sem.at[0], grad_sem.at[1 + n],
              some_entity).wait_recv()
        gt[h, columns, :] = grecv[h * half_lanes : last, columns].astype(F32).T.astype(BF)
        for q in range(cut[0] * nb // 8, cut[1] * nb // 8):
            pl.when(q != mine)(functools.partial(part, h, q))
        if cut[1] == CUTS[-1]:
            frecv[h, mine] = gt[h, my_columns, :]

    panel_out[...] = mm_tn(grad_proj, fetched[...])
    whole(asked_all.at[1:nb], list_sem.at[0], list_sem.at[1], some_bucket).wait()
    for q in range(nb):
        for k in range(HALVES):
            hi = asked_all[q, :, k * half_lanes : (k + 1) * half_lanes] & (LANES - 1)
            hot[k, :, q * half_lanes : (q + 1) * half_lanes] = one_hot(hi, LANES).astype(BF)

    total = None
    for h in range(HALVES):
        for k in range(GROUPS):
            def arrived(count, h=h, k=k):
                whole(frecv.at[h, k * group : k * group + count], part_sem.at[0],
                      part_sem.at[1 + h * GROUPS + k], some_bucket).wait_recv()

            pl.when(my_group == k)(lambda: arrived(group - 1))
            pl.when(my_group != k)(lambda: arrived(group))
            lanes = slice(k * group * half_lanes, (k + 1) * group * half_lanes)
            for q in range(k * group, (k + 1) * group):
                lo = asked_all[q, :, h * half_lanes : (h + 1) * half_lanes] >> 7
                g = frecv[h, q].astype(F32)
                spread[h, :, q * half_lanes : (q + 1) * half_lanes] = jnp.concatenate(
                    [jnp.where(lo == r, g, 0.0) for r in range(high_rows)], axis=0).astype(BF)
            share = mm_nt(spread[h, :, lanes], hot[h, :, lanes])
            total = share if total is None else total + share
    whole(grecv.at[cap:], grad_sem.at[0], grad_sem.at[1], some_entity).wait_send()
    for h in range(HALVES):
        whole(frecv.at[h, 1:nb], part_sem.at[0], part_sem.at[1], some_bucket).wait_send()
    for k in range(high_rows):
        ent_ref[:, k * LANES : (k + 1) * LANES] = total[k * width : (k + 1) * width, :]


def finish(ent_ref, panel_ref, rel_ref, ent_out, panel_out, rel_out, sem):
    outs = [
        pltpu.make_async_copy(src, dst, sem.at[k])
        for k, (src, dst) in enumerate([
            (panel_ref, panel_out), (ent_ref, ent_out), (rel_ref, rel_out)])
    ]
    for out in outs:
        out.start()
    for out in outs:
        out.wait()


def body(ent_table, panels, rel_vecs, head_slots, tail_slots, negatives, requests, block_count):
    nb = lax.axis_size("bucket")
    ne = lax.axis_size("entity")
    rows, feat = ent_table.shape
    cap = requests.shape[2]
    slots = ne * cap
    width = feat // nb
    half = slots // HALVES
    vmem = pl.BlockSpec(memory_space=pltpu.VMEM)
    hbm = pl.BlockSpec(memory_space=pltpu.HBM)
    dma = pltpu.SemaphoreType.DMA
    shapes = (
        jax.ShapeDtypeStruct((width, rows), F32),
        jax.ShapeDtypeStruct((feat, feat), F32),
        jax.ShapeDtypeStruct((1, feat), F32),
    )
    results = pl.pallas_call(
        functools.partial(kernel, nb, ne),
        out_shape=shapes,
        in_specs=[hbm] * 7 + [pl.BlockSpec(memory_space=pltpu.SMEM)],
        out_specs=(vmem,) * 3,
        scratch_shapes=[
            pltpu.VMEM((rows, feat), BF),
            pltpu.VMEM((feat, feat), BF),
            pltpu.VMEM((feat, feat), BF),
            pltpu.VMEM(rel_vecs.shape, BF),
            pltpu.VMEM(head_slots.shape[1:], jnp.int32),
            pltpu.VMEM(tail_slots.shape[1:], jnp.int32),
            pltpu.VMEM(negatives.shape[1:], jnp.int32),
            pltpu.VMEM(requests.shape[1:], jnp.int32),
            pltpu.VMEM((ne, half), jnp.int32),
            pltpu.VMEM((ne, 1, half), jnp.int32),
            pltpu.VMEM((ne, 1, half), jnp.int32),
            pltpu.VMEM((nb, 1, slots), jnp.int32),
            pltpu.VMEM((slots, feat), BF),
            pltpu.VMEM((slots, feat), BF),
            pltpu.VMEM((slots, feat), BF),
            pltpu.VMEM((slots, feat), BF),
            pltpu.VMEM((HALVES, feat, half), BF),
            pltpu.VMEM((HALVES, nb, width, half), BF),
            pltpu.VMEM((HALVES, rows // LANES * width, nb * half), BF),
            pltpu.VMEM((HALVES, LANES, nb * half), BF),
            dma((7,)),
            dma((1 + HALVES,)),
            dma((2,)),
            dma((2,)),
            dma((1 + HALVES * (len(CUTS) - 1),)),
            dma((1 + HALVES * GROUPS,)),
        ],
        compiler_params=pltpu.CompilerParams(
            collective_id=0, has_side_effects=True, vmem_limit_bytes=40 * 1024 * 1024
        ),
        name="transr",
    )(
        *(pltpu.with_memory_space_constraint(x, pltpu.HBM) for x in (
            ent_table, panels[0], rel_vecs, head_slots[0], tail_slots[0], negatives[0],
            requests[0])),
        block_count,
    )
    ent_t, grad_panel, grad_rel = pl.pallas_call(
        finish,
        out_shape=shapes,
        in_specs=[vmem] * 3,
        out_specs=(hbm,) * 3,
        scratch_shapes=[dma((3,))],
        compiler_params=pltpu.CompilerParams(vmem_limit_bytes=8 * 1024 * 1024),
        name="finish",
    )(*results)
    return (ent_t.T, grad_panel[None], grad_rel)


def solution(mesh):
    both = ("bucket", "entity")
    placed = (
        P("entity", None),
        P(both, None, None),
        P(both, None),
        P(both, None, None),
        P(both, None, None),
        P(both, None, None),
        P(both, None, None),
        P(both),
    )
    return jax.shard_map(
        body,
        mesh=mesh,
        in_specs=placed,
        out_specs=(P("entity", "bucket"), P(both, None, None), P(both, None)),
        check_vma=False,
    )
```

```python
import functools

import jax
import jax.numpy as jnp
from jax import lax
from jax.experimental import pallas as pl
from jax.experimental.pallas import tpu as pltpu
from jax.sharding import PartitionSpec as P

MARGIN = 2.0
LANES = 128
HALVES = 2
GROUPS = 4
CUTS = (0, 2, 8)
X_SIZE = 4
MESH = pl.DeviceIdType.MESH
BF = jnp.bfloat16
F32 = jnp.float32


def mm(a, b):
    return jnp.dot(a, b, preferred_element_type=F32)


def mm_nt(a, b):
    return lax.dot_general(a, b, (((1,), (1,)), ((), ())), preferred_element_type=F32)


def mm_tn(a, b):
    return lax.dot_general(a, b, (((0,), (0,)), ((), ())), preferred_element_type=F32)


def iota(shape, axis):
    return lax.broadcasted_iota(jnp.int32, shape, axis)


def to_col(row):
    n = row.shape[1]
    eye = iota((n, n), 0) == iota((n, n), 1)
    return jnp.sum(jnp.where(eye, row, 0.0), axis=1, keepdims=True)


def to_row(col):
    n = col.shape[0]
    eye = iota((n, n), 0) == iota((n, n), 1)
    return jnp.sum(jnp.where(eye, col, 0.0), axis=0, keepdims=True)


def one_hot(row, n):
    return (iota((n, row.shape[1]), 0) == row).astype(F32)


def slot_tables(head_ref, tail_ref, neg_ref, live_count, slots):
    blocks, edge = head_ref.shape
    edges = blocks * edge
    head = jnp.concatenate([head_ref[j : j + 1, :] for j in range(blocks)], axis=1)
    tail = jnp.concatenate([tail_ref[j : j + 1, :] for j in range(blocks)], axis=1)
    head_t = one_hot(head, slots)
    tail_t = one_hot(tail, slots)
    block_of = iota((edges, 1), 0) // edge
    live = (block_of < live_count).astype(F32)
    count = jnp.zeros((edges, slots), F32)
    for j in range(blocks):
        hits = jnp.sum(one_hot(neg_ref[j : j + 1, :], slots), axis=1, keepdims=True)
        count = jnp.where(block_of == j, to_row(hits), count)
    count = count * (live * (1.0 / neg_ref.shape[1]))
    return head_t.astype(BF), tail_t.astype(BF), head_t.T.astype(BF), tail_t.T.astype(BF), live, count


def local_terms(fetched, panel, rel, tables):
    head_t, tail_t, head, tail, live, count = tables
    proj = mm_nt(fetched, panel).astype(BF)
    proj_f = proj.astype(F32)
    centers = (mm(head, proj) + rel).astype(BF)
    center_f = centers.astype(F32)
    offset = center_f - mm(tail, proj)
    pos_weight = jax.nn.sigmoid(jnp.sum(offset * offset, axis=1, keepdims=True) - MARGIN) * live
    proj_sq = to_row(jnp.sum(proj_f * proj_f, axis=1, keepdims=True))
    center_sq = jnp.sum(center_f * center_f, axis=1, keepdims=True)
    dist = center_sq + proj_sq - 2.0 * mm_nt(centers, proj)
    weight = -jax.nn.sigmoid(MARGIN - dist) * count
    weight_t = weight.T
    pulled = 2.0 * pos_weight * offset
    grad_center = (
        pulled
        + 2.0 * jnp.sum(weight, axis=1, keepdims=True) * center_f
        - 2.0 * mm(weight.astype(BF), proj)
    )
    grad_proj = (
        mm(head_t, grad_center.astype(BF))
        - mm(tail_t, pulled.astype(BF))
        + 2.0 * jnp.sum(weight_t, axis=1, keepdims=True) * proj_f
        - 2.0 * mm(weight_t.astype(BF), centers)
    ).astype(BF)
    return grad_proj, jnp.sum(grad_center, axis=0, keepdims=True)


def away(step, size):
    return min(step, size - step)


def kernel(
    nb, ne,
    table_hbm, panel_hbm, rel_hbm, head_hbm, tail_hbm, neg_hbm, req_hbm, count_ref,
    ent_ref, panel_out, rel_out,
    table, panel, panel_q, rel_v, head_v, tail_v, neg_v, req_v, wide,
    msg, reqbuf, asked_all, rows, fetched, gf, grecv, gt, frecv, spread, hot,
    lsem, ask_sem, list_sem, row_sem, grad_sem, part_sem,
):
    b = lax.axis_index("bucket")
    e = lax.axis_index("entity")
    cap = req_v.shape[1]
    slots = ne * cap
    width = frecv.shape[2]
    per_half = ne // HALVES
    half_lanes = per_half * cap
    table_rows = table.shape[0]
    high_rows = table_rows // LANES

    chips = ne // 2
    steps = sorted(range(chips), key=lambda d: away(d, chips))

    def ahead(s):
        return 2 * ((e // 2 + steps[s // 2]) & (chips - 1)) + ((e + s) & 1)

    def behind(s):
        return 2 * ((e // 2 - steps[s // 2]) & (chips - 1)) + ((e + s) & 1)

    zs = nb // X_SIZE
    mine = lax.rem(b, zs) * X_SIZE + b // zs

    far_first = sorted(
        range(1, nb), key=lambda i: -(away(i // zs, X_SIZE) + away(i % zs, zs)))

    def bucket_peer(i):
        return ((b // zs + i // zs) & (X_SIZE - 1)) * zs + ((b + i) & (zs - 1))

    def others(do):
        for q in range(nb):
            pl.when(q != mine)(functools.partial(do, q % X_SIZE * zs + q // X_SIZE))

    some_bucket = {"bucket": lax.rem(b + 1, nb)}
    some_entity = {"entity": lax.rem(e + 1, ne)}

    def signal(where):
        pl.semaphore_signal(barrier, inc=1, device_id=where, device_id_type=MESH)

    def send(src, dst, sent, arrived, where):
        return pltpu.make_async_remote_copy(
            src_ref=src, dst_ref=dst, send_sem=sent, recv_sem=arrived,
            device_id=where, device_id_type=MESH)

    def whole(ref, sent, arrived, where):
        return send(ref, ref, sent, arrived, where)

    loads = [
        pltpu.make_async_copy(src, dst, lsem.at[k])
        for k, (src, dst) in enumerate([
            (req_hbm, req_v), (table_hbm, table), (head_hbm, head_v), (tail_hbm, tail_v),
            (neg_hbm, neg_v), (rel_hbm, rel_v), (panel_hbm, panel),
        ])
    ]
    barrier = pltpu.get_barrier_semaphore()
    loads[0].start()
    for i in far_first:
        signal({"bucket": bucket_peer(i)})
    for s in reversed(range(1, ne)):
        signal({"entity": ahead(s)})
    for load in loads[1:]:
        load.start()

    loads[0].wait()
    req = req_v[...]
    repeat = (iota((cap, half_lanes), 0) == lax.rem(iota((cap, half_lanes), 1), cap)).astype(F32).astype(BF)
    high = mm((req >> 5).astype(F32).astype(BF), repeat)
    low = mm((req & 31).astype(F32).astype(BF), repeat)
    wide[...] = (high * 32.0 + low).astype(jnp.int32)
    for s in range(ne):
        here = iota((1, half_lanes), 1) // cap == s % per_half
        msg[s] = jnp.where(here, wide[pl.ds(ahead(s), 1), :], 0)

    pl.semaphore_wait(barrier, ne + nb - 2)

    for s in reversed(range(1, ne)):
        send(msg.at[s], reqbuf.at[s], ask_sem.at[0], ask_sem.at[1 + s // per_half],
             {"entity": ahead(s)}).start()

    def at_slot(s):
        return slice(s * cap, (s + 1) * cap)

    def at_entity(o):
        return pl.ds(pl.multiple_of(o * cap, cap), cap)

    loads[1].wait()
    for h in range(HALVES):
        first = max(h * per_half, 1)
        last = (h + 1) * per_half
        whole(reqbuf.at[first:last], ask_sem.at[0], ask_sem.at[1 + h], some_entity).wait_recv()
        asked = reqbuf[first] + (reqbuf[first + 1] if h else msg[0])
        for s in range(first + 1 + h, last):
            asked = asked + reqbuf[s]
        asked_all[mine, :, h * half_lanes : last * cap] = asked
        asked_col = to_col(asked.astype(F32)).astype(jnp.int32)
        pick = (iota((half_lanes, table_rows), 1) == asked_col).astype(F32).astype(BF)
        rows[h * half_lanes : last * cap, :] = mm(pick, table[...]).astype(BF)
        for s in reversed(range(first, last)):
            send(rows.at[at_slot(s)], fetched.at[at_entity(e)], row_sem.at[0], row_sem.at[1],
                 {"entity": behind(s)}).start()
    others(lambda peer: send(
        asked_all.at[mine], asked_all.at[mine], list_sem.at[0], list_sem.at[1],
        {"bucket": peer}).start())
    whole(reqbuf.at[1:ne], ask_sem.at[0], ask_sem.at[1], some_entity).wait_send()
    fetched[at_entity(e), :] = rows[at_slot(0), :]

    for load in loads[2:]:
        load.wait()
    feat = panel.shape[1]
    at = iota((feat, feat), 1)
    q_of = at // width
    source = (lax.rem(q_of, X_SIZE) * zs + q_of // X_SIZE) * width + lax.rem(at, width)
    order = (iota((feat, feat), 0) == source).astype(F32).astype(BF)
    panel_q[...] = mm(panel[...], order).astype(BF)
    tables = slot_tables(head_v, tail_v, neg_v, count_ref[0], slots)
    returns = whole(rows.at[cap:], row_sem.at[0], row_sem.at[1], some_entity)
    returns.wait_recv()

    grad_proj, grad_rel = local_terms(fetched[...], panel[...], rel_v[...].astype(F32), tables)
    gf[...] = mm(grad_proj, panel_q[...]).astype(BF)

    pieces = [(cut, h) for cut in zip(CUTS, CUTS[1:]) for h in range(HALVES)]
    for n, (cut, h) in enumerate(pieces):
        columns = slice(cut[0] * nb // 8 * width, cut[1] * nb // 8 * width)
        for s in reversed(range(max(h * per_half, 1), (h + 1) * per_half)):
            send(gf.at[at_entity(ahead(s)), columns], grecv.at[at_slot(s), columns],
                 grad_sem.at[0], grad_sem.at[1 + n], {"entity": ahead(s)}).start()
    grecv[at_slot(0), :] = gf[at_entity(e), :]
    rel_out[...] = grad_rel
    panel_out[...] = mm_tn(grad_proj, fetched[...])
    returns.wait_send()

    group = nb // GROUPS
    my_group = mine // group
    my_columns = pl.ds(pl.multiple_of(mine * width, width), width)
    def part(h, q):
        peer = q % X_SIZE * zs + q // X_SIZE
        send(gt.at[h, q * width : (q + 1) * width, :], frecv.at[h, mine], part_sem.at[0],
             part_sem.at[1 + h * GROUPS + my_group], {"bucket": peer}).start()

    for n, (cut, h) in enumerate(pieces):
        columns = slice(cut[0] * nb // 8 * width, cut[1] * nb // 8 * width)
        first = max(h * half_lanes, cap)
        last = (h + 1) * half_lanes
        whole(grecv.at[first:last, columns], grad_sem.at[0], grad_sem.at[1 + n],
              some_entity).wait_recv()
        gt[h, columns, :] = grecv[h * half_lanes : last, columns].T
        for q in range(cut[0] * nb // 8, cut[1] * nb // 8):
            pl.when(q != mine)(functools.partial(part, h, q))
        if cut[1] == CUTS[-1]:
            frecv[h, mine] = gt[h, my_columns, :]
        if n == 0:
            whole(asked_all.at[1:nb], list_sem.at[0], list_sem.at[1], some_bucket).wait()
            for q in range(nb):
                for k in range(HALVES):
                    hi = asked_all[q, :, k * half_lanes : (k + 1) * half_lanes] & (LANES - 1)
                    hot[k, :, q * half_lanes : (q + 1) * half_lanes] = one_hot(hi, LANES).astype(BF)

    total = None
    for h in range(HALVES):
        for k in range(GROUPS):
            def arrived(count, h=h, k=k):
                whole(frecv.at[h, k * group : k * group + count], part_sem.at[0],
                      part_sem.at[1 + h * GROUPS + k], some_bucket).wait_recv()

            pl.when(my_group == k)(lambda: arrived(group - 1))
            pl.when(my_group != k)(lambda: arrived(group))
            lanes = slice(k * group * half_lanes, (k + 1) * group * half_lanes)
            for q in range(k * group, (k + 1) * group):
                lo = asked_all[q, :, h * half_lanes : (h + 1) * half_lanes] >> 7
                g = frecv[h, q].astype(F32)
                spread[h, :, q * half_lanes : (q + 1) * half_lanes] = jnp.concatenate(
                    [jnp.where(lo == r, g, 0.0) for r in range(high_rows)], axis=0).astype(BF)
            share = mm_nt(spread[h, :, lanes], hot[h, :, lanes])
            total = share if total is None else total + share
    whole(grecv.at[cap:], grad_sem.at[0], grad_sem.at[1], some_entity).wait_send()
    for h in range(HALVES):
        whole(frecv.at[h, 1:nb], part_sem.at[0], part_sem.at[1], some_bucket).wait_send()
    for k in range(high_rows):
        ent_ref[:, k * LANES : (k + 1) * LANES] = total[k * width : (k + 1) * width, :]


def finish(ent_ref, panel_ref, rel_ref, ent_out, panel_out, rel_out, sem):
    outs = [
        pltpu.make_async_copy(src, dst, sem.at[k])
        for k, (src, dst) in enumerate([
            (panel_ref, panel_out), (ent_ref, ent_out), (rel_ref, rel_out)])
    ]
    for out in outs:
        out.start()
    for out in outs:
        out.wait()


def body(ent_table, panels, rel_vecs, head_slots, tail_slots, negatives, requests, block_count):
    nb = lax.axis_size("bucket")
    ne = lax.axis_size("entity")
    rows, feat = ent_table.shape
    cap = requests.shape[2]
    slots = ne * cap
    width = feat // nb
    half = slots // HALVES
    vmem = pl.BlockSpec(memory_space=pltpu.VMEM)
    hbm = pl.BlockSpec(memory_space=pltpu.HBM)
    dma = pltpu.SemaphoreType.DMA
    shapes = (
        jax.ShapeDtypeStruct((width, rows), F32),
        jax.ShapeDtypeStruct((feat, feat), F32),
        jax.ShapeDtypeStruct((1, feat), F32),
    )
    results = pl.pallas_call(
        functools.partial(kernel, nb, ne),
        out_shape=shapes,
        in_specs=[hbm] * 7 + [pl.BlockSpec(memory_space=pltpu.SMEM)],
        out_specs=(vmem,) * 3,
        scratch_shapes=[
            pltpu.VMEM((rows, feat), BF),
            pltpu.VMEM((feat, feat), BF),
            pltpu.VMEM((feat, feat), BF),
            pltpu.VMEM(rel_vecs.shape, BF),
            pltpu.VMEM(head_slots.shape[1:], jnp.int32),
            pltpu.VMEM(tail_slots.shape[1:], jnp.int32),
            pltpu.VMEM(negatives.shape[1:], jnp.int32),
            pltpu.VMEM(requests.shape[1:], jnp.int32),
            pltpu.VMEM((ne, half), jnp.int32),
            pltpu.VMEM((ne, 1, half), jnp.int32),
            pltpu.VMEM((ne, 1, half), jnp.int32),
            pltpu.VMEM((nb, 1, slots), jnp.int32),
            pltpu.VMEM((slots, feat), BF),
            pltpu.VMEM((slots, feat), BF),
            pltpu.VMEM((slots, feat), BF),
            pltpu.VMEM((slots, feat), BF),
            pltpu.VMEM((HALVES, feat, half), BF),
            pltpu.VMEM((HALVES, nb, width, half), BF),
            pltpu.VMEM((HALVES, rows // LANES * width, nb * half), BF),
            pltpu.VMEM((HALVES, LANES, nb * half), BF),
            dma((7,)),
            dma((1 + HALVES,)),
            dma((2,)),
            dma((2,)),
            dma((1 + HALVES * (len(CUTS) - 1),)),
            dma((1 + HALVES * GROUPS,)),
        ],
        compiler_params=pltpu.CompilerParams(
            collective_id=0, has_side_effects=True, vmem_limit_bytes=40 * 1024 * 1024
        ),
        name="transr",
    )(
        *(pltpu.with_memory_space_constraint(x, pltpu.HBM) for x in (
            ent_table, panels[0], rel_vecs, head_slots[0], tail_slots[0], negatives[0],
            requests[0])),
        block_count,
    )
    ent_t, grad_panel, grad_rel = pl.pallas_call(
        finish,
        out_shape=shapes,
        in_specs=[vmem] * 3,
        out_specs=(hbm,) * 3,
        scratch_shapes=[dma((3,))],
        compiler_params=pltpu.CompilerParams(vmem_limit_bytes=8 * 1024 * 1024),
        name="finish",
    )(*results)
    return (ent_t.T, grad_panel[None], grad_rel)


def solution(mesh):
    both = ("bucket", "entity")
    placed = (
        P("entity", None),
        P(both, None, None),
        P(both, None),
        P(both, None, None),
        P(both, None, None),
        P(both, None, None),
        P(both, None, None),
        P(both),
    )
    return jax.shard_map(
        body,
        mesh=mesh,
        in_specs=placed,
        out_specs=(P("entity", "bucket"), P(both, None, None), P(both, None)),
        check_vma=False,
    )
```
